256 devices in a mesh: expert: 64 (over y, z, core), dp: 4 (over x).
Axes of the slice: x: 4, y: 4, z: 8, core: 2. Of those that a mesh axis runs over, the one named last changes fastest.
Arguments:
- tokens: bfloat16 [8192, 2048], P(('expert', 'dp')), may hold values from -6 to 6
- expert_ids: int32 [8192, 8], P(('expert', 'dp')), may hold values from 0 to 63, all different within a row; in each aligned block of 32 rows (0 to 31, 32 to 63, ...) at most 8 rows name the same one
- gate_weights: bfloat16 [8192, 8], P(('expert', 'dp')), may hold values from 0.049804688 to 0.25
- cotangent: bfloat16 [8192, 2048], P(('expert', 'dp')), may hold values from -12 to 12
- w_gate: bfloat16 [64, 768, 2048], P('expert'), may hold values from -0.125 to 0.125
- w_up: bfloat16 [64, 768, 2048], P('expert'), may hold values from -0.125 to 0.125
- w_down: bfloat16 [64, 2048, 768], P('expert'), may hold values from -0.21875 to 0.21875
Outputs:
- token_grad: bfloat16 [8192, 2048], P(('expert', 'dp'))
- gate_grad: bfloat16 [8192, 8], P(('expert', 'dp'))
- grad_gate: bfloat16 [64, 768, 2048], P('expert', 'dp')
- grad_up: bfloat16 [64, 768, 2048], P('expert', 'dp')
- grad_down_t: bfloat16 [64, 768, 2048], P('expert', 'dp')
The draws below stay inside these ranges and needn't reach their ends.
Inputs may be any that keep to these rules, and one draw needn't show every extreme that they name: `expert_ids`: each token names 8 different experts. Among the tokens of one device (aligned blocks of 32 rows), no expert is named by more than 8 of them, a bound that some block reaches.
All inputs are finite; a program needn't handle non-finite values.
Results may differ from the reference program's by a relative error of at most 0.017.
Values may be sent and summed in bfloat16 or wider, within the bound.
A program may use at most 128 MiB of HBM per device.

```python
import math
import jax
import jax.numpy as jnp
import numpy as np
from jax import lax

D = 2048
H = 768
TOP = 8
TOK_DEV = 32
EXPERTS = 64
CAP = 8
TOKENS = 8192
N_EXPERT = 64
N_DP = 4


def steps_of(key, dims, shards, smallest, largest):
    def one(dim, shards_of):
        heights = jax.random.uniform(jax.random.fold_in(jax.random.fold_in(key, 6), dim), (shards_of,), jnp.float32, smallest / len(shards), largest / len(shards))
        return jnp.repeat(jnp.exp(heights), dims[dim] // shards_of).reshape((-1,) + (1,) * (len(dims) - dim - 1))

    level = one(*shards[0])
    for cut in shards[1:]:
        level = level * one(*cut)
    return level


def routed_block(rng, own, number, rows, count, top, bound, skew):
    sequence = jax.random.permutation(rng, count)
    packed, ordinary = shares(count, rows * top, bound, skew, True), shares(count, rows * top, bound, skew, False)
    places = jnp.arange(count)

    def named(sizes, rotation):
        used = int((sizes > 0).sum())
        fixed = max(1, used // 4)
        shifted = fixed + (places - fixed + rotation * (used - fixed)) % max(1, count - fixed)
        return jnp.zeros((count,), jnp.int32).at[sequence[jnp.where(places < fixed, places, shifted)]].set(jnp.asarray(sizes, jnp.int32))

    sizes = jnp.where(number % 4 == 0, named(packed, number // 4), named(ordinary, number - number // 4 - 1))
    mixed = jax.random.permutation(jax.random.fold_in(own, 3), count)
    source_of, taker = mixed[0:count // 2 * 2:2], mixed[1:count // 2 * 2:2]
    margin = jnp.minimum(sizes[source_of] - 1, bound - sizes[taker]) // 2
    margin = jnp.where((source_of == sequence[0]) | (taker == sequence[0]) | (sizes[taker] == 0), 0, jnp.maximum(margin, 0))
    shifted = jax.random.randint(jax.random.fold_in(own, 4), (count // 2,), 0, 1 << 20) % (margin + 1)
    sizes = sizes.at[source_of].add(-shifted).at[taker].add(shifted)
    items = jnp.searchsorted(jnp.cumsum(sizes), jnp.arange(rows * top), side="right").astype(jnp.int32)
    table = items.reshape(top, rows).T
    table = table[jax.random.permutation(jax.random.fold_in(own, 1), rows)]
    rotation = jax.random.randint(jax.random.fold_in(own, 2), (rows, 1), 0, top)
    return jnp.take_along_axis(table, (jnp.arange(top)[None, :] + rotation) % top, axis=1)


def shares(number_of, total, most, lean, full):
    weights = [(1 << 20) // math.isqrt(rank ** lean) + 1 for rank in range(1, number_of + 1)]
    largest = most if full else min(most, max(-(-total // number_of), total * weights[0] // sum(weights)))
    least = 1 if total - largest >= number_of - 1 else 0
    counts, surplus = [largest] + [least] * (number_of - 1), total - largest - least * (number_of - 1)
    while surplus > 0:
        free = [i for i in range(1, number_of) if counts[i] < largest] or [i for i in range(1, number_of) if counts[i] < most]
        mass, budget = sum([weights[i] for i in free]), surplus
        for i in free:
            more = min(most - counts[i], max(1, budget * weights[i] // mass), surplus)
            counts[i] = counts[i] + more
            surplus = surplus - more
    return np.array(counts)


def centred(rng, shape, width, limit, pieces=(), kind=jnp.bfloat16):
    entries = jax.random.normal(rng, shape, jnp.float32) * width
    if len(pieces) > 0:
        entries = steps_of(rng, shape, pieces, -0.22, 0.18) * entries
    return jnp.clip(entries, min=-limit, max=limit).astype(kind)


def setup_inputs(seed: int = 0) -> dict:
    seeds = jax.random.split(jax.random.key(seed), 8)
    tokens = centred(seeds[0], (TOKENS, D), 1.0, 6.0, ((0, 256),))
    expert_ids_keys = jax.random.split(jax.random.fold_in(seeds[1], 1), TOKENS // TOK_DEV)
    expert_ids_turns = jax.random.permutation(jax.random.fold_in(seeds[1], 3), TOKENS // TOK_DEV)
    expert_ids = jax.vmap(lambda own, number: routed_block(jax.random.fold_in(seeds[1], 2), own, number, TOK_DEV, EXPERTS, TOP, CAP, 2))(expert_ids_keys, expert_ids_turns).reshape((TOKENS, TOP))
    gate_weights = jnp.clip(0.049804688 + 0.20019531 * jax.random.uniform(seeds[2], (TOKENS, TOP), jnp.float32) ** steps_of(seeds[2], (TOKENS, TOP), ((0, 256),), -0.2, 0.2), 0.049804688, 0.25).astype(jnp.bfloat16)
    cotangent = centred(seeds[3], (TOKENS, D), 2.0, 12.0, ((0, 256),))
    w_gate = centred(seeds[4], (EXPERTS, H, D), D ** -0.5, 0.125, ((0, 64),))
    w_up = centred(seeds[5], (EXPERTS, H, D), D ** -0.5, 0.125, ((0, 64),))
    w_down = centred(seeds[6], (EXPERTS, D, H), H ** -0.5, 0.21875, ((0, 64),))
    return dict(tokens=tokens, expert_ids=expert_ids, gate_weights=gate_weights, cotangent=cotangent, w_gate=w_gate, w_up=w_up, w_down=w_down)


def contract_last(left, right):
    return lax.dot_general(left, right, (((1,), (1,)), ((), ())), preferred_element_type=jnp.float32)


def contract_first(left, right):
    return lax.dot_general(left, right, (((0,), (0,)), ((), ())), preferred_element_type=jnp.float32)


def rounded(value):
    return lax.optimization_barrier(value.astype(jnp.bfloat16)).astype(jnp.float32)


def expert_forward(expert_rows, gate_mat, up_mat, down_mat):
    pre_gate = contract_last(expert_rows, gate_mat)
    pre_up = contract_last(expert_rows, up_mat)
    gate_sigmoid = jax.nn.sigmoid(pre_gate)
    hidden = (pre_gate * gate_sigmoid * pre_up).astype(jnp.bfloat16)
    outputs = contract_last(hidden, down_mat).astype(jnp.bfloat16)
    return pre_gate, pre_up, gate_sigmoid, hidden, outputs


def reference(tokens, expert_ids, gate_weights, cotangent, w_gate, w_up, w_down):
    blocks = TOKENS // TOK_DEV
    slot_count = TOK_DEV * TOP
    buffer_rows = N_EXPERT * CAP
    block_ids = expert_ids.reshape(blocks, slot_count)
    onehot = (block_ids[:, :, None] == jnp.arange(EXPERTS, dtype=jnp.int32)[None, None, :]).astype(jnp.int32)
    slot_rank = jnp.sum((jnp.cumsum(onehot, axis=1) - 1) * onehot, axis=2).astype(jnp.int32)
    block_index = jnp.arange(blocks, dtype=jnp.int32)[:, None] * jnp.ones((1, slot_count), jnp.int32)
    group_index = block_index % N_DP
    source_index = block_index // N_DP
    slot_index = block_index * slot_count + jnp.arange(slot_count, dtype=jnp.int32)[None, :]
    table = jnp.full((N_DP, EXPERTS, N_EXPERT, CAP), -1, jnp.int32)
    table = table.at[group_index, block_ids, source_index, slot_rank].set(slot_index)
    table_by_expert = jnp.transpose(table, (1, 0, 2, 3))
    flat_gates = gate_weights.reshape(-1)

    def per_expert(carry, inputs):
        token_acc, score_acc = carry
        gate_mat, up_mat, down_mat, entry = inputs
        sums = [jnp.zeros((H, D), jnp.float32) for _ in range(3)]
        for group_id in range(N_DP):
            index = entry[group_id].reshape(buffer_rows)
            valid = index >= 0
            safe = jnp.maximum(index, 0).astype(jnp.int32)
            token_id = (safe // TOP).astype(jnp.int32)
            expert_rows = jnp.where(valid[:, None], tokens[token_id], jnp.zeros((), jnp.bfloat16))
            cot_rows = cotangent[token_id]
            gate_rows = jnp.where(valid, flat_gates[safe].astype(jnp.float32), jnp.zeros((), jnp.float32))
            pre_gate, pre_up, gate_sigmoid, hidden, outputs = expert_forward(expert_rows, gate_mat, up_mat, down_mat)
            score = jnp.sum(outputs.astype(jnp.float32) * cot_rows.astype(jnp.float32), axis=1)
            scaled = (gate_rows[:, None] * cot_rows.astype(jnp.float32)).astype(jnp.bfloat16)
            d_hidden = jnp.dot(scaled, down_mat, preferred_element_type=jnp.float32)
            d_pre_gate = (d_hidden * pre_up * gate_sigmoid * (1.0 + pre_gate * (1.0 - gate_sigmoid))).astype(jnp.bfloat16)
            d_pre_up = (d_hidden * pre_gate * gate_sigmoid).astype(jnp.bfloat16)
            slot_grad = (jnp.dot(d_pre_gate, gate_mat, preferred_element_type=jnp.float32)
                         + jnp.dot(d_pre_up, up_mat, preferred_element_type=jnp.float32)).astype(jnp.bfloat16)
            token_acc = token_acc.at[token_id].add(jnp.where(valid[:, None], slot_grad.astype(jnp.float32), jnp.zeros((), jnp.float32)))
            score_acc = score_acc.at[safe].add(jnp.where(valid, score, jnp.zeros((), jnp.float32)))
            sums[0] = sums[0] + rounded(contract_first(d_pre_gate, expert_rows))
            sums[1] = sums[1] + rounded(contract_first(d_pre_up, expert_rows))
            sums[2] = sums[2] + rounded(contract_first(hidden, scaled))
        return (token_acc, score_acc), (sums[0].astype(jnp.bfloat16), sums[1].astype(jnp.bfloat16), sums[2].astype(jnp.bfloat16))

    start = (jnp.zeros((TOKENS, D), jnp.float32), jnp.zeros((TOKENS * TOP,), jnp.float32))
    (token_acc, score_acc), (grad_gate, grad_up, grad_down_t) = lax.scan(
        per_expert, start, (w_gate, w_up, w_down, table_by_expert))
    token_grad = token_acc.astype(jnp.bfloat16)
    gate_grad = score_acc.reshape(TOKENS, TOP).astype(jnp.bfloat16)
    return (token_grad, gate_grad, grad_gate, grad_up, grad_down_t)
```

```python
import jax
import jax.numpy as jnp
from jax import lax
from jax.sharding import PartitionSpec as P


def contract_last(left, right):
    return lax.dot_general(
        left, right, (((1,), (1,)), ((), ())), preferred_element_type=jnp.float32
    )


def contract_first(left, right):
    return lax.dot_general(
        left, right, (((0,), (0,)), ((), ())), preferred_element_type=jnp.float32
    )


def rounded(value):
    return lax.optimization_barrier(value.astype(jnp.bfloat16)).astype(jnp.float32)


def expert_forward(expert_rows, gate_mat, up_mat, down_mat):
    pre_gate = contract_last(expert_rows, gate_mat)
    pre_up = contract_last(expert_rows, up_mat)
    gate_sigmoid = jax.nn.sigmoid(pre_gate)
    hidden = (pre_gate * gate_sigmoid * pre_up).astype(jnp.bfloat16)
    outputs = contract_last(hidden, down_mat).astype(jnp.bfloat16)
    return (pre_gate, pre_up, gate_sigmoid, hidden, outputs)


def body(tokens, expert_ids, gate_weights, cotangent, w_gate, w_up, w_down):
    tok_rows, top_count = expert_ids.shape
    model_width = tokens.shape[1]
    experts = lax.axis_size("expert")
    capacity = min(tok_rows, 2 * tok_rows * top_count // experts)
    slot_count = tok_rows * top_count
    buffer_rows = experts * capacity
    flat_ids = expert_ids.reshape(slot_count)
    order = jnp.arange(slot_count, dtype=jnp.int32)
    earlier = (flat_ids[:, None] == flat_ids[None, :]) & (order[None, :] < order[:, None])
    slot_rank = jnp.sum(earlier.astype(jnp.int32), axis=1)
    position = flat_ids * capacity + slot_rank
    placing = (jnp.arange(buffer_rows, dtype=jnp.int32)[:, None] == position[None, :]).astype(
        jnp.bfloat16
    )
    token_map = placing.reshape(buffer_rows, tok_rows, top_count).sum(axis=2)
    x_send = jnp.dot(token_map, tokens, preferred_element_type=jnp.float32).astype(jnp.bfloat16)
    x_send = x_send.reshape(experts, capacity, model_width)
    cot_send = jnp.dot(token_map, cotangent, preferred_element_type=jnp.float32).astype(
        jnp.bfloat16
    )
    cot_send = cot_send.reshape(experts, capacity, model_width)
    gate_send = jnp.dot(
        placing, gate_weights.reshape(slot_count), preferred_element_type=jnp.float32
    )
    gate_send = gate_send.astype(jnp.bfloat16).reshape(experts, capacity)
    gate_mat = w_gate[0]
    up_mat = w_up[0]
    down_mat = w_down[0]
    x_recv = lax.all_to_all(x_send, "expert", split_axis=0, concat_axis=0, tiled=True)
    expert_rows = x_recv.reshape(buffer_rows, model_width)
    pre_gate, pre_up, gate_sigmoid, hidden, outputs = expert_forward(
        expert_rows, gate_mat, up_mat, down_mat
    )
    cot_recv, gate_recv = (
        lax.all_to_all(cot_send, "expert", split_axis=0, concat_axis=0, tiled=True),
        lax.all_to_all(gate_send, "expert", split_axis=0, concat_axis=0, tiled=True),
    )
    cot_rows = cot_recv.reshape(buffer_rows, model_width)
    gate_rows = gate_recv.reshape(buffer_rows).astype(jnp.float32)
    scaled = (gate_rows[:, None] * cot_rows.astype(jnp.float32)).astype(jnp.bfloat16)
    d_hidden = jnp.dot(scaled, down_mat, preferred_element_type=jnp.float32)
    d_pre_gate = (
        d_hidden * pre_up * gate_sigmoid * (1.0 + pre_gate * (1.0 - gate_sigmoid))
    ).astype(jnp.bfloat16)
    d_pre_up = (d_hidden * pre_gate * gate_sigmoid).astype(jnp.bfloat16)
    slot_grad = (
        jnp.dot(d_pre_gate, gate_mat, preferred_element_type=jnp.float32)
        + jnp.dot(d_pre_up, up_mat, preferred_element_type=jnp.float32)
    ).astype(jnp.bfloat16)
    pieces = []
    for operand, partner in ((d_pre_gate, expert_rows), (d_pre_up, expert_rows), (hidden, scaled)):
        pieces.append(rounded(contract_first(operand, partner)))
    summed = lax.psum_scatter(
        jnp.concatenate(pieces, axis=1).astype(jnp.bfloat16), "dp", scatter_dimension=0, tiled=True
    ).astype(jnp.float32)
    grad_gate = summed[:, :model_width].astype(jnp.bfloat16)[None]
    grad_up = summed[:, model_width : 2 * model_width].astype(jnp.bfloat16)[None]
    grad_down_t = summed[:, 2 * model_width :].astype(jnp.bfloat16)[None]
    slot_back = slot_grad.reshape(experts, capacity, model_width)
    out_send = outputs.reshape(experts, capacity, model_width)
    grad_back, out_back = (
        lax.all_to_all(slot_back, "expert", split_axis=0, concat_axis=0, tiled=True),
        lax.all_to_all(out_send, "expert", split_axis=0, concat_axis=0, tiled=True),
    )
    picked = out_back.reshape(buffer_rows, model_width)[position].astype(jnp.float32)
    picked = picked.reshape(tok_rows, top_count, model_width)
    gate_grad = jnp.sum(picked * cotangent.astype(jnp.float32)[:, None, :], axis=2).astype(
        jnp.bfloat16
    )
    gathered = grad_back.reshape(buffer_rows, model_width)[position].astype(jnp.float32)
    token_grad = gathered.reshape(tok_rows, top_count, model_width).sum(axis=1).astype(jnp.bfloat16)
    return (token_grad, gate_grad, grad_gate, grad_up, grad_down_t)


def solution(mesh):
    return jax.shard_map(
        body,
        mesh=mesh,
        in_specs=(
            P(("expert", "dp"), None),
            P(("expert", "dp"), None),
            P(("expert", "dp"), None),
            P(("expert", "dp"), None),
            P("expert", None, None),
            P("expert", None, None),
            P("expert", None, None),
        ),
        out_specs=(
            P(("expert", "dp"), None),
            P(("expert", "dp"), None),
            P("expert", "dp", None),
            P("expert", "dp", None),
            P("expert", "dp", None),
        ),
        check_vma=False,
    )
```

```python
import jax
import jax.numpy as jnp
from jax import lax
from jax.sharding import PartitionSpec as P

F32 = jnp.float32
BF16 = jnp.bfloat16
LANES = 128


def contract_last(left, right):
    return lax.dot_general(
        left, right, (((1,), (1,)), ((), ())), preferred_element_type=F32
    )


def contract_first(left, right):
    return lax.dot_general(
        left, right, (((0,), (0,)), ((), ())), preferred_element_type=F32
    )


def body(tokens, expert_ids, gate_weights, cotangent, w_gate, w_up, w_down):
    tok_rows, top_count = expert_ids.shape
    model_width = tokens.shape[1]
    experts = lax.axis_size("expert")
    capacity = min(tok_rows, 2 * tok_rows * top_count // experts)
    slot_count = tok_rows * top_count
    buffer_rows = experts * capacity
    flat_ids = expert_ids.reshape(slot_count)
    order = jnp.arange(slot_count, dtype=jnp.int32)
    earlier = (flat_ids[:, None] == flat_ids[None, :]) & (order[None, :] < order[:, None])
    slot_rank = jnp.sum(earlier.astype(jnp.int32), axis=1)
    position = (flat_ids * capacity + slot_rank).reshape(tok_rows, top_count)
    row = jnp.arange(buffer_rows, dtype=jnp.int32)
    hit = [row[:, None] == position[None, :, k] for k in range(top_count)]
    gates = gate_weights.astype(F32)
    token_map = sum(h.astype(F32) for h in hit).astype(BF16)
    gate_map = sum(jnp.where(h, gates[None, :, k], 0.0) for k, h in enumerate(hit)).astype(BF16)
    x_send = jnp.dot(token_map, tokens, preferred_element_type=F32).astype(BF16)
    x_send = x_send.reshape(experts, capacity, model_width)
    scaled_send = jnp.dot(gate_map, cotangent, preferred_element_type=F32).astype(BF16)
    scaled_send = scaled_send.reshape(experts, capacity, model_width)
    gate_mat = w_gate[0]
    up_mat = w_up[0]
    down_mat = w_down[0]
    x_rows = lax.all_to_all(x_send, "expert", split_axis=0, concat_axis=0, tiled=True)
    x_rows = x_rows.reshape(buffer_rows, model_width)
    pre_gate = contract_last(x_rows, gate_mat)
    pre_up = contract_last(x_rows, up_mat)
    sig = jax.nn.sigmoid(pre_gate)
    hidden32 = pre_gate * sig * pre_up
    hidden = hidden32.astype(BF16)
    scaled = lax.all_to_all(scaled_send, "expert", split_axis=0, concat_axis=0, tiled=True)
    scaled = scaled.reshape(buffer_rows, model_width)
    d_hidden = jnp.dot(scaled, down_mat, preferred_element_type=F32)
    d_pre_gate = (d_hidden * pre_up * sig * (1.0 + pre_gate * (1.0 - sig))).astype(BF16)
    d_pre_up = (d_hidden * pre_gate * sig).astype(BF16)
    slot_score = jnp.sum(hidden.astype(F32) * d_hidden, axis=1)
    slot_grad = (
        jnp.dot(d_pre_gate, gate_mat, preferred_element_type=F32)
        + jnp.dot(d_pre_up, up_mat, preferred_element_type=F32)
    ).astype(BF16)
    pieces = [
        contract_first(operand, partner).astype(BF16)
        for operand, partner in ((d_pre_gate, x_rows), (d_pre_up, x_rows), (hidden, scaled))
    ]
    summed = lax.psum_scatter(
        jnp.concatenate(pieces, axis=1), "dp", scatter_dimension=0, tiled=True
    )
    grad_gate = summed[:, :model_width][None]
    grad_up = summed[:, model_width : 2 * model_width][None]
    grad_down_t = summed[:, 2 * model_width :][None]
    high = slot_score.astype(BF16)
    low = (slot_score - high.astype(F32)).astype(BF16)
    lane = jnp.arange(LANES, dtype=jnp.int32)[None, :]
    extra = jnp.where(lane == 0, high[:, None], jnp.where(lane == 1, low[:, None], 0).astype(BF16))
    back = jnp.concatenate([slot_grad, extra], axis=1).reshape(
        experts, capacity, model_width + LANES
    )
    back = lax.all_to_all(back, "expert", split_axis=0, concat_axis=0, tiled=True)
    back = back.reshape(buffer_rows, model_width + LANES)
    token_grad = contract_first(token_map, back[:, :model_width]).astype(BF16)
    score = back[:, model_width].astype(F32) + back[:, model_width + 1].astype(F32)
    scores = jnp.stack(
        [jnp.sum(jnp.where(h, score[:, None], 0.0), axis=0) for h in hit], axis=1
    )
    gate_grad = (scores / gates).astype(BF16)
    return (token_grad, gate_grad, grad_gate, grad_up, grad_down_t)


def solution(mesh):
    rows = P(("expert", "dp"), None)
    whole = P("expert", None, None)
    split = P("expert", "dp", None)
    return jax.shard_map(
        body,
        mesh=mesh,
        in_specs=(rows, rows, rows, rows, whole, whole, whole),
        out_specs=(rows, rows, split, split, split),
        check_vma=False,
    )
```

```python
import functools

import jax
import jax.numpy as jnp
from jax import lax
from jax.experimental import pallas as pl
from jax.experimental.pallas import tpu as pltpu
from jax.sharding import PartitionSpec as P

F32 = jnp.float32
BF16 = jnp.bfloat16
LANES = 128
MESH = pl.DeviceIdType.MESH
YS, ZS = 4, 8
GROUP = 8


def contract_last(left, right):
    return lax.dot_general(
        left, right, (((1,), (1,)), ((), ())), preferred_element_type=F32
    )


def contract_first(left, right):
    return lax.dot_general(
        left, right, (((0,), (0,)), ((), ())), preferred_element_type=F32
    )


def dot(left, right):
    return jnp.dot(left, right, preferred_element_type=F32)


def expert_kernel(
    cap,
    tok_ref,
    meta_ref,
    cot_ref,
    wg_hbm,
    wu_hbm,
    wd_hbm,
    rows_ref,
    scaled_ref,
    hidden_ref,
    dgate_ref,
    dup_ref,
    back_ref,
    xg,
    cg,
    wg,
    wu,
    wd,
    pre_gate,
    pre_up,
    x_send,
    x_recv,
    c_send,
    c_recv,
    w_sem,
):
    e = lax.axis_index("expert")
    dp = lax.axis_index("dp")
    core = e % 2
    z = (e // 2) % ZS
    y = e // (2 * ZS)
    turn = 1 - 2 * core
    toks, width = tok_ref.shape
    sources = xg.shape[0]
    hid = wg.shape[0]
    rows = sources * cap

    loads = [
        pltpu.make_async_copy(src.at[0], dst, w_sem.at[i])
        for i, (src, dst) in enumerate(((wg_hbm, wg), (wu_hbm, wu), (wd_hbm, wd)))
    ]
    for load in loads:
        load.start()

    def yat(j):
        return (y + j) % YS

    def zat(k):
        return (z + turn * k + 2 * ZS) % ZS

    def place(j, k, c=core):
        return (yat(j) * ZS + zat(k)) * 2 + c

    ahead, behind, partner = place(0, 1), place(0, -1), place(0, 0, 1 - core)
    across = [place(j, 0) for j in range(1, YS)]
    barrier = pltpu.get_barrier_semaphore()
    for peer in (ahead, behind, partner, *across):
        pl.semaphore_signal(barrier, inc=1, device_id=(peer, dp), device_id_type=MESH)

    xg[e, :, :width] = tok_ref[...]
    xg[e, :, width:] = meta_ref[...]
    cg[e] = cot_ref[...]
    pl.semaphore_wait(barrier, 3 + len(across))

    sends = []
    used = {"x": 0, "c": 0}

    def push(kind, block, peers):
        buf, ssem, rsem = (xg, x_send, x_recv) if kind == "x" else (cg, c_send, c_recv)
        for peer in peers:
            copy = pltpu.make_async_remote_copy(
                src_ref=buf.at[block],
                dst_ref=buf.at[block],
                send_sem=ssem.at[used[kind]],
                recv_sem=rsem.at[block],
                device_id=(peer, dp),
                device_id_type=MESH,
            )
            copy.start()
            used[kind] += 1
            sends.append(copy)

    def arrived(kind, block):
        buf, ssem, rsem = (xg, x_send, x_recv) if kind == "x" else (cg, c_send, c_recv)
        pltpu.make_async_remote_copy(
            src_ref=buf.at[block],
            dst_ref=buf.at[block],
            send_sem=ssem.at[0],
            recv_sem=rsem.at[block],
            device_id=(partner, dp),
            device_id_type=MESH,
        ).wait_recv()

    far = ZS // 2

    def x_step(j, k):
        block = place(j, k)
        arrived("x", block)
        on = []
        if k == 0:
            on = [ahead, behind]
        elif -far < k < 0:
            on = [ahead]
        elif 0 < k < far - 1:
            on = [behind]
        push("x", block, [*on, partner])

    def c_step(k):
        block = place(0, k)
        arrived("c", block)
        on = []
        if -far < k < 0:
            on = [ahead]
        elif 0 < k < far - 1:
            on = [behind]
        push("c", block, [*on, *across, partner])

    def c_hand(j, k):
        block = place(j, k)
        arrived("c", block)
        push("c", block, [partner])

    push("x", e, [*across, ahead, behind])
    push("c", e, [ahead, behind, *across])
    push("x", e, [partner])
    push("c", e, [partner])
    for j in range(1, YS):
        x_step(j, 0)
    for k in range(1, far + 1):
        signs = (-1, 1) if k < far else (-1,)
        for sign in signs:
            c_step(sign * k)
        for j in range(1, YS):
            for sign in (-1, 1) if k > 1 else (1,):
                c_hand(j, sign * (k - 1))
        for j in range(YS):
            for sign in signs:
                x_step(j, sign * k)
    for j in range(1, YS):
        c_hand(j, -far)

    for k in range(-far, far):
        for j in range(YS):
            arrived("x", place(j, k, 1 - core))
    group_tokens = GROUP * toks
    group_rows = GROUP * cap
    before = lax.broadcasted_iota(jnp.int32, (group_tokens, group_tokens), 0)
    after = lax.broadcasted_iota(jnp.int32, (group_tokens, group_tokens), 1)
    earlier = ((before < after) & (before // toks == after // toks)).astype(F32).astype(BF16)
    row = lax.broadcasted_iota(jnp.int32, (group_rows, group_tokens), 0)
    col = lax.broadcasted_iota(jnp.int32, (group_rows, group_tokens), 1)
    own_block = row // cap == col // toks
    slot = (row % cap).astype(F32)
    lane = lax.broadcasted_iota(jnp.int32, (group_tokens, LANES), 1)
    mine = e.astype(F32)
    ones = jnp.ones((8, LANES), BF16)
    top = 8

    def select(g):
        block = pl.ds(g * GROUP, GROUP)
        meta = xg[block, :, width:].reshape(group_tokens, LANES).astype(F32)
        named = (meta == mine) & (lane < top)
        gate = jnp.where(named, pltpu.roll(meta, LANES - top, 1), 0.0).astype(BF16)
        hits = jnp.where(named, 1.0, 0.0).astype(BF16)
        here = contract_last(ones, hits)
        rank = dot(here.astype(BF16), earlier)
        weight = contract_last(ones, gate)[0:1]
        chosen = own_block & (here[0:1] > 0.5) & (rank[0:1] == slot)
        return chosen, weight

    def pick_x(g, _):
        chosen, _w = select(g)
        tokens = xg[pl.ds(g * GROUP, GROUP), :, :width].reshape(group_tokens, width)
        one_hot = jnp.where(chosen, 1.0, 0.0).astype(BF16)
        start = pl.multiple_of(g * group_rows, group_rows)
        rows_ref[pl.ds(start, group_rows), :] = dot(one_hot, tokens).astype(BF16)
        return 0

    lax.fori_loop(0, sources // GROUP, pick_x, 0)

    tile = 256
    loads[0].wait()
    loads[1].wait()

    def forward(n, _):
        cols = pl.ds(pl.multiple_of(n * tile, tile), tile)
        pre_gate[n] = contract_last(rows_ref[...], wg[cols, :])
        pre_up[n] = contract_last(rows_ref[...], wu[cols, :])
        return 0

    lax.fori_loop(0, hid // tile, forward, 0)

    for k in range(-far, far):
        for j in range(YS):
            arrived("c", place(j, k, 1 - core))

    def pick_c(g, _):
        chosen, weight = select(g)
        cots = cg[pl.ds(g * GROUP, GROUP)].reshape(group_tokens, width)
        one_gate = jnp.where(chosen, weight, 0.0).astype(BF16)
        start = pl.multiple_of(g * group_rows, group_rows)
        scaled_ref[pl.ds(start, group_rows), :] = dot(one_gate, cots).astype(BF16)
        return 0

    lax.fori_loop(0, sources // GROUP, pick_c, 0)
    loads[2].wait()

    score = jnp.zeros((rows, 1), F32)
    for n in range(hid // tile):
        cols = pl.ds(n * tile, tile)
        d_hidden = dot(scaled_ref[...], wd[:, cols])
        gate, up = pre_gate[n], pre_up[n]
        sig = jax.nn.sigmoid(gate)
        act = gate * sig
        hidden = (act * up).astype(BF16)
        hidden_ref[:, cols] = hidden
        dgate_ref[:, cols] = (d_hidden * up * sig * (1.0 + gate * (1.0 - sig))).astype(BF16)
        dup_ref[:, cols] = (d_hidden * act).astype(BF16)
        score += jnp.sum(hidden.astype(F32) * d_hidden, axis=1, keepdims=True)

    high = score.astype(BF16).astype(F32)
    out_lane = lax.broadcasted_iota(jnp.int32, (rows, LANES), 1)
    extra = jnp.where(out_lane == 0, high, jnp.where(out_lane == 1, score - high, 0.0))
    back_ref[:, width:] = extra.astype(BF16)

    def backward(n, _):
        cols = pl.ds(pl.multiple_of(n * tile, tile), tile)
        total = dot(dgate_ref[...], wg[:, cols]) + dot(dup_ref[...], wu[:, cols])
        back_ref[:, cols] = total.astype(BF16)
        return 0

    lax.fori_loop(0, width // tile, backward, 0)

    for copy in sends:
        copy.wait_send()


def expert_call(tokens, meta, cotangent, w_gate, w_up, w_down, cap):
    toks, width = tokens.shape
    sources = lax.axis_size("expert")
    hid = w_gate.shape[1]
    rows = sources * cap
    tiles = hid // 256
    vmem = pl.BlockSpec(memory_space=pltpu.VMEM)
    hbm = pl.BlockSpec(memory_space=pl.ANY)
    copies = 63 if YS == 4 and ZS == 8 else 0
    shape = jax.ShapeDtypeStruct
    return pl.pallas_call(
        functools.partial(expert_kernel, cap),
        out_shape=(
            shape((rows, width), BF16),
            shape((rows, width), BF16),
            shape((rows, hid), BF16),
            shape((rows, hid), BF16),
            shape((rows, hid), BF16),
            shape((rows, width + LANES), BF16),
        ),
        in_specs=[vmem, vmem, vmem, hbm, hbm, hbm],
        out_specs=[vmem] * 6,
        scratch_shapes=[
            pltpu.VMEM((sources, toks, width + LANES), BF16),
            pltpu.VMEM((sources, toks, width), BF16),
            pltpu.VMEM((hid, width), BF16),
            pltpu.VMEM((hid, width), BF16),
            pltpu.VMEM((width, hid), BF16),
            pltpu.VMEM((tiles, rows, 256), F32),
            pltpu.VMEM((tiles, rows, 256), F32),
            pltpu.SemaphoreType.DMA((copies,)),
            pltpu.SemaphoreType.DMA((sources,)),
            pltpu.SemaphoreType.DMA((copies,)),
            pltpu.SemaphoreType.DMA((sources,)),
            pltpu.SemaphoreType.DMA((3,)),
        ],
        compiler_params=pltpu.CompilerParams(
            collective_id=0, has_side_effects=True, vmem_limit_bytes=60 << 20
        ),
    )(tokens, meta, cotangent, w_gate, w_up, w_down)


def body(tokens, expert_ids, gate_weights, cotangent, w_gate, w_up, w_down):
    tok_rows, top_count = expert_ids.shape
    width = tokens.shape[1]
    experts = lax.axis_size("expert")
    cap = min(tok_rows, 2 * tok_rows * top_count // experts)
    buffer_rows = experts * cap
    meta = jnp.concatenate(
        [
            expert_ids.astype(BF16),
            gate_weights,
            jnp.zeros((tok_rows, LANES - 2 * top_count), BF16),
        ],
        axis=1,
    )
    x_rows, scaled, hidden, d_pre_gate, d_pre_up, back = expert_call(
        tokens, meta, cotangent, w_gate, w_up, w_down, cap
    )
    pieces = [
        contract_first(operand, partner).astype(BF16)
        for operand, partner in ((d_pre_gate, x_rows), (d_pre_up, x_rows), (hidden, scaled))
    ]
    summed = lax.psum_scatter(
        jnp.concatenate(pieces, axis=1), "dp", scatter_dimension=0, tiled=True
    )
    grad_gate = summed[:, :width][None]
    grad_up = summed[:, width : 2 * width][None]
    grad_down_t = summed[:, 2 * width :][None]

    slot_count = tok_rows * top_count
    flat_ids = expert_ids.reshape(slot_count)
    order = jnp.arange(slot_count, dtype=jnp.int32)
    earlier = (flat_ids[:, None] == flat_ids[None, :]) & (order[None, :] < order[:, None])
    slot_rank = jnp.sum(earlier.astype(jnp.int32), axis=1)
    position = (flat_ids * cap + slot_rank).reshape(tok_rows, top_count)
    row = jnp.arange(buffer_rows, dtype=jnp.int32)
    hit = [row[:, None] == position[None, :, k] for k in range(top_count)]
    token_map = sum(h.astype(F32) for h in hit).astype(BF16)

    back = lax.all_to_all(
        back.reshape(experts, cap, width + LANES), "expert", split_axis=0, concat_axis=0, tiled=True
    )
    back = back.reshape(buffer_rows, width + LANES)
    token_grad = contract_first(token_map, back[:, :width]).astype(BF16)
    score = back[:, width].astype(F32) + back[:, width + 1].astype(F32)
    scores = jnp.stack(
        [jnp.sum(jnp.where(h, score[:, None], 0.0), axis=0) for h in hit], axis=1
    )
    gate_grad = (scores / gate_weights.astype(F32)).astype(BF16)
    return (token_grad, gate_grad, grad_gate, grad_up, grad_down_t)


def solution(mesh):
    rows = P(("expert", "dp"), None)
    whole = P("expert", None, None)
    split = P("expert", "dp", None)
    return jax.shard_map(
        body,
        mesh=mesh,
        in_specs=(rows, rows, rows, rows, whole, whole, whole),
        out_specs=(rows, rows, split, split, split),
        check_vma=False,
    )
```

```python
import functools

import jax
import jax.numpy as jnp
from jax import lax
from jax.experimental import pallas as pl
from jax.experimental.pallas import tpu as pltpu
from jax.sharding import PartitionSpec as P

F32 = jnp.float32
BF16 = jnp.bfloat16
LANES = 128
MESH = pl.DeviceIdType.MESH
YS, ZS = 4, 8
GROUP = ZS


def contract_last(left, right):
    return lax.dot_general(
        left, right, (((1,), (1,)), ((), ())), preferred_element_type=F32
    )


def contract_first(left, right):
    return lax.dot_general(
        left, right, (((0,), (0,)), ((), ())), preferred_element_type=F32
    )


def dot(left, right):
    return jnp.dot(left, right, preferred_element_type=F32)


def expert_kernel(
    cap,
    tok_ref,
    meta_ref,
    cot_ref,
    wg_hbm,
    wu_hbm,
    wd_hbm,
    grad_ref,
    home_ref,
    xg,
    cg,
    wg,
    wu,
    wd,
    wd_t,
    pre_gate,
    pre_up,
    pair,
    left,
    d_gate,
    d_up,
    back,
    first,
    ring,
    x_send,
    x_recv,
    c_send,
    c_recv,
    home_send,
    home_recv,
    ring_send,
    ring_recv,
    w_sem,
):
    e = lax.axis_index("expert")
    dp = lax.axis_index("dp")
    core = e % 2
    z = (e // 2) % ZS
    y = e // (2 * ZS)
    turn = 1 - 2 * core
    toks, width = tok_ref.shape
    sources = xg.shape[0]
    hid = wg.shape[0]
    rows = sources * cap
    half_rows = rows // 2
    far = ZS // 2
    group_tokens = GROUP * toks
    group_rows = GROUP * cap
    ring_size = ring.shape[0] + 1
    owned = hid // ring_size
    parts = ring.shape[2]
    cut = ring.shape[4]

    loads = [
        pltpu.make_async_copy(src.at[0], dst, w_sem.at[i])
        for i, (src, dst) in enumerate(((wd_hbm, wd), (wg_hbm, wg), (wu_hbm, wu)))
    ]
    for load in loads:
        load.start()

    def yat(j):
        return (y + j) % YS

    def zat(k):
        return (z + turn * k + 2 * ZS) % ZS

    def place(j, k, c=core):
        return (yat(j) * ZS + zat(k)) * 2 + c

    ahead, behind, partner = place(0, 1), place(0, -1), place(0, 0, 1 - core)
    across = [place(j, 0) for j in range(1, YS)]
    ring_to = ((dp + 1) % ring_size, (dp + ring_size - 1) % ring_size)
    barrier = pltpu.get_barrier_semaphore()
    for peer in ring_to:
        pl.semaphore_signal(barrier, inc=1, device_id=(e, peer), device_id_type=MESH)

    def greet(i, _):
        peer = (e + i) % sources
        pl.semaphore_signal(barrier, inc=1, device_id=(peer, dp), device_id_type=MESH)
        return 0

    lax.fori_loop(1, sources, greet, 0)
    xg[e, :, :width] = tok_ref[...]
    xg[e, :, width:] = meta_ref[...]
    cg[e] = cot_ref[...]
    pl.semaphore_wait(barrier, sources - 1 + 2)

    sends = []
    used = {"x": 0, "c": 0}

    def push(kind, block, peers):
        buf, ssem, rsem = (xg, x_send, x_recv) if kind == "x" else (cg, c_send, c_recv)
        for peer in peers:
            copy = pltpu.make_async_remote_copy(
                src_ref=buf.at[block],
                dst_ref=buf.at[block],
                send_sem=ssem.at[used[kind]],
                recv_sem=rsem.at[block],
                device_id=(peer, dp),
                device_id_type=MESH,
            )
            copy.start()
            used[kind] += 1
            sends.append(copy)

    def arrived(kind, block):
        buf, ssem, rsem = (xg, x_send, x_recv) if kind == "x" else (cg, c_send, c_recv)
        pltpu.make_async_remote_copy(
            src_ref=buf.at[block],
            dst_ref=buf.at[block],
            send_sem=ssem.at[0],
            recv_sem=rsem.at[block],
            device_id=(partner, dp),
            device_id_type=MESH,
        ).wait_recv()

    def x_step(j, k):
        block = place(j, k)
        arrived("x", block)
        on = []
        if k == 0:
            on = [ahead, behind]
        elif -far < k < 0:
            on = [ahead]
        elif 0 < k < far - 1:
            on = [behind]
        push("x", block, [*on, partner])

    def c_step(k):
        block = place(0, k)
        arrived("c", block)
        on = []
        if -far < k < 0:
            on = [ahead]
        elif 0 < k < far - 1:
            on = [behind]
        push("c", block, [*on, *across, partner])

    def c_hand(j, k):
        block = place(j, k)
        arrived("c", block)
        push("c", block, [partner])

    before = lax.broadcasted_iota(jnp.int32, (group_tokens, group_tokens), 0)
    after = lax.broadcasted_iota(jnp.int32, (group_tokens, group_tokens), 1)
    earlier = ((before < after) & (before // toks == after // toks)).astype(F32).astype(BF16)
    row = lax.broadcasted_iota(jnp.int32, (group_rows, group_tokens), 0)
    col = lax.broadcasted_iota(jnp.int32, (group_rows, group_tokens), 1)
    own_block = row // cap == col // toks
    slot = (row % cap).astype(F32)
    lane = lax.broadcasted_iota(jnp.int32, (group_tokens, LANES), 1)
    mine = e.astype(F32)
    ones = jnp.ones((8, LANES), BF16)
    top = 8
    tile = 256
    tiles = hid // tile

    def select(g):
        block = pl.ds(g * GROUP, GROUP)
        meta = xg[block, :, width:].reshape(group_tokens, LANES).astype(F32)
        named = (meta == mine) & (lane < top)
        gate = jnp.where(named, pltpu.roll(meta, LANES - top, 1), 0.0).astype(BF16)
        hits = jnp.where(named, 1.0, 0.0).astype(BF16)
        here = contract_last(ones, hits)
        rank = dot(here.astype(BF16), earlier)
        weight = contract_last(ones, gate)[0:1]
        chosen = own_block & (here[0:1] > 0.5) & (rank[0:1] == slot)
        return chosen, weight

    def handed(kind, half):
        for j in range(YS):
            for i in range(far):
                arrived(kind, (j * ZS + half * far + i) * 2 + 1 - core)

    def take_x(half):
        handed("x", half)
        base = pl.multiple_of(half * half_rows, half_rows)

        def pick(j, _):
            g = 2 * j + half
            chosen, _w = select(g)
            tokens = xg[pl.ds(g * GROUP, GROUP), :, :width].reshape(group_tokens, width)
            one_hot = jnp.where(chosen, 1.0, 0.0).astype(BF16)
            start = pl.multiple_of(base + j * group_rows, group_rows)
            pair[0, pl.ds(start, group_rows), :] = dot(one_hot, tokens).astype(BF16)
            return 0

        lax.fori_loop(0, YS, pick, 0)
        span = pl.ds(base, half_rows)

        def forward(n, _):
            cols = pl.ds(pl.multiple_of(n * tile, tile), tile)
            pre_gate[n, :, span] = contract_last(wg[cols, :], pair[0, span, :])
            pre_up[n, :, span] = contract_last(wu[cols, :], pair[0, span, :])
            return 0

        lax.fori_loop(0, tiles, forward, 0)

    def take_c(half):
        handed("c", half)
        base = pl.multiple_of(half * half_rows, half_rows)

        def pick(j, _):
            g = 2 * j + half
            chosen, weight = select(g)
            cots = cg[pl.ds(g * GROUP, GROUP)].reshape(group_tokens, width)
            one_gate = jnp.where(chosen, weight, 0.0).astype(BF16)
            start = pl.multiple_of(base + j * group_rows, group_rows)
            pair[1, pl.ds(start, group_rows), :] = dot(one_gate, cots).astype(BF16)
            return 0

        lax.fori_loop(0, YS, pick, 0)
        span = pl.ds(base, half_rows)

        def grads(n, score):
            cols = pl.ds(pl.multiple_of(n * tile, tile), tile)
            d_hidden = contract_last(wd_t[cols, :], pair[1, span, :])
            gate, up = pre_gate[n, :, span], pre_up[n, :, span]
            sig = jax.nn.sigmoid(gate)
            act = gate * sig
            hidden = (act * up).astype(BF16)
            left[0, cols, span] = hidden
            left[1, cols, span] = (
                d_hidden * up * sig * (1.0 + gate * (1.0 - sig))
            ).astype(BF16)
            left[2, cols, span] = (d_hidden * act).astype(BF16)
            return score + jnp.sum(hidden.astype(F32) * d_hidden, axis=0, keepdims=True)

        score = lax.fori_loop(0, tiles, grads, jnp.zeros((1, half_rows), F32))
        high = score.astype(BF16).astype(F32)
        which = lax.broadcasted_iota(jnp.int32, (8, half_rows), 0)
        both = jnp.where(which == 0, high, jnp.where(which == 1, score - high, 0.0))
        unit = lax.broadcasted_iota(jnp.int32, (8, LANES), 0) == lax.broadcasted_iota(
            jnp.int32, (8, LANES), 1
        )
        unit = jnp.where(unit, 1.0, 0.0).astype(BF16)
        back[span, width:] = contract_first(both.astype(BF16), unit).astype(BF16)

    def turn_down(c):
        span = pl.ds(c * tile, tile)
        wd_t[:, span] = wd[span, :].T

    push("x", e, [*across, ahead, behind])
    push("c", e, [ahead, behind, *across])
    push("x", e, [partner])
    push("c", e, [partner])
    turns = list(range(width // tile))
    loads[0].wait()
    turn_down(turns.pop())
    for j in range(1, YS):
        x_step(j, 0)
    own_half = z // far
    for k in range(1, far + 1):
        signs = (-1, 1) if k < far else (-1,)
        for sign in signs:
            c_step(sign * k)
        for j in range(1, YS):
            for sign in (-1, 1) if k > 1 else (1,):
                c_hand(j, sign * (k - 1))
        for j in range(YS):
            for sign in signs:
                x_step(j, sign * k)
            if turns:
                turn_down(turns.pop())
        if k == far - 1:
            while turns:
                turn_down(turns.pop())
            loads[1].wait()
            loads[2].wait()
            take_x(own_half)
    take_x(1 - own_half)
    for j in range(1, YS):
        c_hand(j, -far)
    take_c(own_half)
    take_c(1 - own_half)

    owners = [
        [(dp + ring_size - 1 - s) % ring_size for s in range(ring_size)],
        [(dp + 1 + s) % ring_size for s in range(ring_size)],
    ]

    def partial(owner, side, i):
        per = parts // 3
        m = i // per
        cols = pl.ds(pl.multiple_of((side * per + i % per) * cut, cut), cut)
        lhs = left[m, pl.ds(pl.multiple_of(owner * owned, 16), owned), :]
        return dot(lhs, pair[(3 - m) // 3, :, cols]), m, cols

    def ring_copy(s, side, i):
        return pltpu.make_async_remote_copy(
            src_ref=first.at[side, i] if s == 0 else ring.at[s - 1, side, i],
            dst_ref=ring.at[s, side, i],
            send_sem=ring_send.at[s, side, i],
            recv_sem=ring_recv.at[s, side, i],
            device_id=(e, ring_to[side]),
            device_id_type=MESH,
        )

    def ring_start(i, _):
        for side in range(2):
            first[side, i] = partial(owners[side][0], side, i)[0].astype(BF16)
            ring_copy(0, side, i).start()
        return 0

    lax.fori_loop(0, parts, ring_start, 0)

    for n in range(tiles):
        span = pl.ds(n * tile, tile)
        d_gate[:, span] = left[1, span, :].T
        d_up[:, span] = left[2, span, :].T

    def backward(n, _):
        cols = pl.ds(pl.multiple_of(n * tile, tile), tile)
        total = dot(d_gate[...], wg[:, cols]) + dot(d_up[...], wu[:, cols])
        back[:, cols] = total.astype(BF16)
        return 0

    lax.fori_loop(0, width // tile, backward, 0)

    def home_at(s):
        half = (s // 2) % ZS // far
        g = half * YS + s // (2 * ZS)
        return pl.multiple_of(g * group_rows + s % GROUP * cap, cap)

    def home_copy(peer):
        return pltpu.make_async_remote_copy(
            src_ref=back.at[pl.ds(home_at(peer), cap), :],
            dst_ref=home_ref.at[pl.ds(pl.multiple_of(e * cap, cap), cap), :],
            send_sem=home_send.at[peer],
            recv_sem=home_recv.at[e],
            device_id=(peer, dp),
            device_id_type=MESH,
        )

    def go_home(i, _):
        home_copy((e + i) % sources).start()
        return 0

    lax.fori_loop(1, sources, go_home, 0)
    kept = pltpu.make_async_copy(
        back.at[pl.ds(home_at(e), cap), :],
        home_ref.at[pl.ds(pl.multiple_of(e * cap, cap), cap), :],
        w_sem.at[3],
    )
    kept.start()

    for s in range(1, ring_size - 1):

        def ring_on(i, _):
            for side in range(2):
                ring_copy(s - 1, side, i).wait_recv()
                mine_now = partial(owners[side][s], side, i)[0]
                ring[s - 1, side, i] = (mine_now + ring[s - 1, side, i].astype(F32)).astype(BF16)
                ring_copy(s, side, i).start()
            return 0

        lax.fori_loop(0, parts, ring_on, 0)

    last = ring_size - 2

    def ring_end(i, _):
        for side in range(2):
            ring_copy(last, side, i).wait_recv()
            total, m, cols = partial(dp, side, i)
            grad_ref[m, :, cols] = (total + ring[last, side, i].astype(F32)).astype(BF16)
        return 0

    lax.fori_loop(0, parts, ring_end, 0)

    kept.wait()

    def came_home(i, _):
        peer = (e + i) % sources
        pltpu.make_async_remote_copy(
            src_ref=back.at[pl.ds(0, cap), :],
            dst_ref=home_ref.at[pl.ds(pl.multiple_of(peer * cap, cap), cap), :],
            send_sem=home_send.at[peer],
            recv_sem=home_recv.at[peer],
            device_id=(peer, dp),
            device_id_type=MESH,
        ).wait_recv()
        home_copy(peer).wait_send()
        return 0

    lax.fori_loop(1, sources, came_home, 0)
    for s in range(ring_size - 1):

        def ring_sent(i, _):
            for side in range(2):
                ring_copy(s, side, i).wait_send()
            return 0

        lax.fori_loop(0, parts, ring_sent, 0)
    for copy in sends:
        copy.wait_send()


def expert_call(tokens, meta, cotangent, w_gate, w_up, w_down, cap):
    toks, width = tokens.shape
    sources = lax.axis_size("expert")
    ring_size = lax.axis_size("dp")
    hid = w_gate.shape[1]
    rows = sources * cap
    tiles = hid // 256
    owned = hid // ring_size
    per = 2
    cut = width // (2 * per)
    parts = 3 * per
    far = ZS // 2
    x_copies = 6 + YS - 4 + 3 * (YS - 1) + YS * (4 * far - 4)
    c_copies = YS + 2 + far * YS + far - 1 + (far - 1) * YS + far - 2 + (YS - 1) * ZS
    vmem = pl.BlockSpec(memory_space=pltpu.VMEM)
    hbm = pl.BlockSpec(memory_space=pl.ANY)
    shape = jax.ShapeDtypeStruct
    dma = pltpu.SemaphoreType.DMA
    return pl.pallas_call(
        functools.partial(expert_kernel, cap),
        out_shape=(
            shape((3, owned, width), BF16),
            shape((rows, width + LANES), BF16),
        ),
        in_specs=[vmem, vmem, vmem, hbm, hbm, hbm],
        out_specs=[vmem] * 2,
        scratch_shapes=[
            pltpu.VMEM((sources, toks, width + LANES), BF16),
            pltpu.VMEM((sources, toks, width), BF16),
            pltpu.VMEM((hid, width), BF16),
            pltpu.VMEM((hid, width), BF16),
            pltpu.VMEM((width, hid), BF16),
            pltpu.VMEM((hid, width), BF16),
            pltpu.VMEM((tiles, 256, rows), F32),
            pltpu.VMEM((tiles, 256, rows), F32),
            pltpu.VMEM((2, rows, width), BF16),
            pltpu.VMEM((3, hid, rows), BF16),
            pltpu.VMEM((rows, hid), BF16),
            pltpu.VMEM((rows, hid), BF16),
            pltpu.VMEM((rows, width + LANES), BF16),
            pltpu.VMEM((2, parts, owned, cut), BF16),
            pltpu.VMEM((ring_size - 1, 2, parts, owned, cut), BF16),
            dma((x_copies,)),
            dma((sources,)),
            dma((c_copies,)),
            dma((sources,)),
            dma((sources,)),
            dma((sources,)),
            dma((ring_size - 1, 2, parts)),
            dma((ring_size - 1, 2, parts)),
            dma((4,)),
        ],
        compiler_params=pltpu.CompilerParams(
            collective_id=0, has_side_effects=True, vmem_limit_bytes=60 << 20
        ),
    )(tokens, meta, cotangent, w_gate, w_up, w_down)


def body(tokens, expert_ids, gate_weights, cotangent, w_gate, w_up, w_down):
    tok_rows, top_count = expert_ids.shape
    width = tokens.shape[1]
    experts = lax.axis_size("expert")
    cap = min(tok_rows, 2 * tok_rows * top_count // experts)
    buffer_rows = experts * cap
    meta = jnp.concatenate(
        [
            expert_ids.astype(BF16),
            gate_weights,
            jnp.zeros((tok_rows, LANES - 2 * top_count), BF16),
        ],
        axis=1,
    )
    grads, back = expert_call(tokens, meta, cotangent, w_gate, w_up, w_down, cap)
    grad_down_t, grad_gate, grad_up = grads[0:1], grads[1:2], grads[2:3]

    slot_count = tok_rows * top_count
    flat_ids = expert_ids.reshape(slot_count)
    order = jnp.arange(slot_count, dtype=jnp.int32)
    earlier = (flat_ids[:, None] == flat_ids[None, :]) & (order[None, :] < order[:, None])
    slot_rank = jnp.sum(earlier.astype(jnp.int32), axis=1)
    position = (flat_ids * cap + slot_rank).reshape(tok_rows, top_count)
    row = jnp.arange(buffer_rows, dtype=jnp.int32)
    hit = [row[:, None] == position[None, :, k] for k in range(top_count)]
    token_map = sum(h.astype(F32) for h in hit).astype(BF16)

    token_grad = contract_first(token_map, back[:, :width]).astype(BF16)
    score = back[:, width].astype(F32) + back[:, width + 1].astype(F32)
    scores = jnp.stack(
        [jnp.sum(jnp.where(h, score[:, None], 0.0), axis=0) for h in hit], axis=1
    )
    gate_grad = (scores / gate_weights.astype(F32)).astype(BF16)
    return (token_grad, gate_grad, grad_gate, grad_up, grad_down_t)


def solution(mesh):
    rows = P(("expert", "dp"), None)
    whole = P("expert", None, None)
    split = P("expert", "dp", None)
    return jax.shard_map(
        body,
        mesh=mesh,
        in_specs=(rows, rows, rows, rows, whole, whole, whole),
        out_specs=(rows, rows, split, split, split),
        check_vma=False,
    )
```

```python
import functools

import jax
import jax.numpy as jnp
from jax import lax
from jax.experimental import pallas as pl
from jax.experimental.pallas import tpu as pltpu
from jax.sharding import PartitionSpec as P

F32 = jnp.float32
BF16 = jnp.bfloat16
LANES = 128
MESH = pl.DeviceIdType.MESH
YS, ZS = 4, 8
GROUP = 2 * YS


def contract_last(left, right):
    return lax.dot_general(
        left, right, (((1,), (1,)), ((), ())), preferred_element_type=F32
    )


def contract_first(left, right):
    return lax.dot_general(
        left, right, (((0,), (0,)), ((), ())), preferred_element_type=F32
    )


def dot(left, right):
    return jnp.dot(left, right, preferred_element_type=F32)


def expert_kernel(
    cap,
    tok_ref,
    ids_ref,
    gates_ref,
    cot_ref,
    wg_hbm,
    wu_hbm,
    wd_hbm,
    tok_out,
    gate_out,
    down_out,
    gate_mat_out,
    up_out,
    xg,
    cg,
    wg,
    wu,
    wd,
    wd_t,
    pre_gate,
    pre_up,
    pair,
    left,
    d_gate,
    d_up,
    back,
    home_ref,
    first,
    ring,
    x_send,
    x_recv,
    c_send,
    c_recv,
    home_send,
    home_recv,
    ring_send,
    ring_recv,
    w_sem,
):
    e = lax.axis_index("expert")
    dp = lax.axis_index("dp")
    core = e % 2
    z = (e // 2) % ZS
    y = e // (2 * ZS)
    turn = 1 - 2 * core
    toks, width = tok_ref.shape
    sources = xg.shape[0]
    hid = wg.shape[0]
    rows = sources * cap
    half_rows = rows // 2
    far = ZS // 2
    group_tokens = GROUP * toks
    group_rows = GROUP * cap
    ring_size = ring.shape[0] + 1
    owned = hid // ring_size
    parts = ring.shape[2]
    cut = ring.shape[4]
    top = ids_ref.shape[0]

    loads = [
        pltpu.make_async_copy(src.at[0], dst, w_sem.at[i])
        for i, (src, dst) in enumerate(((wd_hbm, wd), (wg_hbm, wg), (wu_hbm, wu)))
    ]
    for load in loads:
        load.start()

    def device(j, k, q):
        return ((y + turn * j + YS) % YS * ZS + (z + turn * k + ZS) % ZS) * 2 + (core + q) % 2

    def spot(j, k, q=0):
        return ((k + far // 2) % ZS * YS + j % YS) * 2 + q

    hops = {
        "ahead": (device(0, 1, 0), 0, -1),
        "behind": (device(0, -1, 0), 0, 1),
        "up": (device(1, 0, 0), -1, 0),
        "down": (device(-1, 0, 0), 1, 0),
    }
    partner = device(0, 0, 1)
    ring_to = ((dp + 1) % ring_size, (dp + ring_size - 1) % ring_size)
    barrier = pltpu.get_barrier_semaphore()
    for peer in ring_to:
        pl.semaphore_signal(barrier, inc=1, device_id=(e, peer), device_id_type=MESH)

    def greet(i, _):
        peer = (e + i) % sources
        pl.semaphore_signal(barrier, inc=1, device_id=(peer, dp), device_id_type=MESH)
        return 0

    lax.fori_loop(1, sources, greet, 0)
    named_here = jnp.concatenate([ids_ref[...].astype(F32), gates_ref[...].astype(F32)], axis=0)
    unit16 = lax.broadcasted_iota(jnp.int32, (2 * top, LANES), 0) == lax.broadcasted_iota(
        jnp.int32, (2 * top, LANES), 1
    )
    unit16 = jnp.where(unit16, 1.0, 0.0).astype(BF16)
    meta_own = contract_first(named_here.astype(BF16), unit16)
    own = spot(0, 0)
    xg[own, :, :width] = tok_ref[...]
    xg[own, :, width:] = meta_own.astype(BF16)
    cg[own] = cot_ref[...]
    pl.semaphore_wait(barrier, sources - 1 + 2)

    sends = []
    used = {"x": 0, "c": 0}

    def push(kind, j, k, ways):
        buf, ssem, rsem = (xg, x_send, x_recv) if kind == "x" else (cg, c_send, c_recv)
        for way in ways:
            if way == "partner":
                peer, there = partner, spot(-j, -k, 1)
            else:
                peer, dj, dk = hops[way]
                there = spot(j + dj, k + dk)
            copy = pltpu.make_async_remote_copy(
                src_ref=buf.at[spot(j, k)],
                dst_ref=buf.at[there],
                send_sem=ssem.at[used[kind]],
                recv_sem=rsem.at[there],
                device_id=(peer, dp),
                device_id_type=MESH,
            )
            copy.start()
            used[kind] += 1
            sends.append(copy)

    def arrived(kind, slot_at):
        buf, ssem, rsem = (xg, x_send, x_recv) if kind == "x" else (cg, c_send, c_recv)
        pltpu.make_async_remote_copy(
            src_ref=buf.at[slot_at],
            dst_ref=buf.at[slot_at],
            send_sem=ssem.at[0],
            recv_sem=rsem.at[slot_at],
            device_id=(partner, dp),
            device_id_type=MESH,
        ).wait_recv()

    def along_z(k):
        if -far < k < 0:
            return ["ahead"]
        return ["behind"] if 0 < k < far - 1 else []

    def x_step(j, k):
        arrived("x", spot(j, k))
        ways = ["ahead", "behind"] if k == 0 else along_z(k)
        if k == 0 and j == -1:
            ways = ["up", *ways]
        push("x", j, k, [*ways, "partner"])

    def c_step(k):
        arrived("c", spot(0, k))
        push("c", 0, k, [*along_z(k), "up", "down", "partner"])

    def c_hand(j, k):
        arrived("c", spot(j, k))
        push("c", j, k, ["up", "partner"] if j == -1 else ["partner"])

    before = lax.broadcasted_iota(jnp.int32, (group_tokens, group_tokens), 0)
    after = lax.broadcasted_iota(jnp.int32, (group_tokens, group_tokens), 1)
    earlier = ((before < after) & (before // toks == after // toks)).astype(F32).astype(BF16)
    row = lax.broadcasted_iota(jnp.int32, (group_rows, group_tokens), 0)
    col = lax.broadcasted_iota(jnp.int32, (group_rows, group_tokens), 1)
    own_block = row // cap == col // toks
    slot = (row % cap).astype(F32)
    lane = lax.broadcasted_iota(jnp.int32, (group_tokens, LANES), 1)
    mine = e.astype(F32)
    ones = jnp.ones((8, LANES), BF16)
    tile = 256
    tiles = hid // tile

    def select(g):
        block = pl.ds(g * GROUP, GROUP)
        meta = xg[block, :, width:].reshape(group_tokens, LANES).astype(F32)
        named = (meta == mine) & (lane < top)
        gate = jnp.where(named, pltpu.roll(meta, LANES - top, 1), 0.0).astype(BF16)
        hits = jnp.where(named, 1.0, 0.0).astype(BF16)
        here = contract_last(ones, hits)
        rank = dot(here.astype(BF16), earlier)
        weight = contract_last(ones, gate)[0:1]
        chosen = own_block & (here[0:1] > 0.5) & (rank[0:1] == slot)
        return chosen, weight

    def handed(kind, half):
        for k in range(-(far // 2), far // 2):
            for j in range(YS):
                arrived(kind, spot(j, k + half * far, 1))

    def take_x(half):
        handed("x", half)
        base = half * half_rows

        def pick(j, _):
            g = half * (sources // GROUP // 2) + j
            chosen, _w = select(g)
            tokens = xg[pl.ds(g * GROUP, GROUP), :, :width].reshape(group_tokens, width)
            one_hot = jnp.where(chosen, 1.0, 0.0).astype(BF16)
            start = pl.multiple_of(base + j * group_rows, group_rows)
            pair[0, pl.ds(start, group_rows), :] = dot(one_hot, tokens).astype(BF16)
            return 0

        lax.fori_loop(0, sources // GROUP // 2, pick, 0)
        span = pl.ds(base, half_rows)

        def forward(n, _):
            cols = pl.ds(pl.multiple_of(n * tile, tile), tile)
            pre_gate[n, :, span] = contract_last(wg[cols, :], pair[0, span, :])
            pre_up[n, :, span] = contract_last(wu[cols, :], pair[0, span, :])
            return 0

        lax.fori_loop(0, tiles, forward, 0)

    def take_c(half):
        handed("c", half)
        base = half * half_rows

        def pick(j, _):
            g = half * (sources // GROUP // 2) + j
            chosen, weight = select(g)
            cots = cg[pl.ds(g * GROUP, GROUP)].reshape(group_tokens, width)
            one_gate = jnp.where(chosen, weight, 0.0).astype(BF16)
            start = pl.multiple_of(base + j * group_rows, group_rows)
            pair[1, pl.ds(start, group_rows), :] = dot(one_gate, cots).astype(BF16)
            return 0

        lax.fori_loop(0, sources // GROUP // 2, pick, 0)
        span = pl.ds(base, half_rows)

        def grads(n, score):
            cols = pl.ds(pl.multiple_of(n * tile, tile), tile)
            d_hidden = contract_last(wd_t[cols, :], pair[1, span, :])
            gate, up = pre_gate[n, :, span], pre_up[n, :, span]
            sig = jax.nn.sigmoid(gate)
            act = gate * sig
            hidden = (act * up).astype(BF16)
            left[0, cols, span] = hidden
            left[1, cols, span] = (
                d_hidden * up * sig * (1.0 + gate * (1.0 - sig))
            ).astype(BF16)
            left[2, cols, span] = (d_hidden * act).astype(BF16)
            return score + jnp.sum(hidden.astype(F32) * d_hidden, axis=0, keepdims=True)

        score = lax.fori_loop(0, tiles, grads, jnp.zeros((1, half_rows), F32))
        high = score.astype(BF16).astype(F32)
        which = lax.broadcasted_iota(jnp.int32, (8, half_rows), 0)
        both = jnp.where(which == 0, high, jnp.where(which == 1, score - high, 0.0))
        unit = lax.broadcasted_iota(jnp.int32, (8, LANES), 0) == lax.broadcasted_iota(
            jnp.int32, (8, LANES), 1
        )
        unit = jnp.where(unit, 1.0, 0.0).astype(BF16)
        back[span, width:] = contract_first(both.astype(BF16), unit).astype(BF16)

    def turn_down(c):
        span = pl.ds(c * tile, tile)
        wd_t[:, span] = wd[span, :].T

    push("x", 0, 0, ["up", "down", "ahead", "behind"])
    push("c", 0, 0, ["ahead", "behind", "up", "down"])
    push("x", 0, 0, ["partner"])
    push("c", 0, 0, ["partner"])
    turns = list(range(width // tile))
    loads[0].wait()
    turn_down(turns.pop())
    for j in (-1, 1, -2):
        x_step(j, 0)

    def both_ways(k):
        return (0,) if k == 0 else (-k, k) if k < far else (-k,)

    def c_turn(at):
        for k in range(far + 1):
            if k > 0 and at == k + 1:
                for way in both_ways(k):
                    c_step(way)
            if at == k + 3:
                for way in both_ways(k):
                    c_hand(-1, way)
                    c_hand(1, way)
            if at == k + 4:
                for way in both_ways(k):
                    c_hand(-2, way)

    for k in range(1, far + 1):
        for h, js in enumerate(((0, -1), (1, -2))):
            c_turn(2 * k + h)
            for j in js:
                for way in both_ways(k):
                    x_step(j, way)
                if turns:
                    turn_down(turns.pop())
        if k == far // 2:
            loads[1].wait()
            loads[2].wait()
            take_x(0)
        if k < far and 2 * k + 1 >= far // 2 + 4:
            while turns:
                turn_down(turns.pop())
            take_c(0)
    for at in range(2 * far + 2, far + 5):
        c_turn(at)
    while turns:
        turn_down(turns.pop())
    take_x(1)
    if 2 * far - 1 < far // 2 + 4:
        take_c(0)
    take_c(1)

    owners = [
        [(dp + ring_size - 1 - s) % ring_size for s in range(ring_size)],
        [(dp + 1 + s) % ring_size for s in range(ring_size)],
    ]

    def partial(owner, side, i):
        per = parts // 3
        m = i // per
        cols = pl.ds(pl.multiple_of((side * per + i % per) * cut, cut), cut)
        lhs = left[m, pl.ds(pl.multiple_of(owner * owned, 16), owned), :]
        return dot(lhs, pair[(3 - m) // 3, :, cols]), m, cols

    def ring_copy(s, side, i):
        return pltpu.make_async_remote_copy(
            src_ref=first.at[side, i] if s == 0 else ring.at[s - 1, side, i],
            dst_ref=ring.at[s, side, i],
            send_sem=ring_send.at[s, side, i],
            recv_sem=ring_recv.at[s, side, i],
            device_id=(e, ring_to[side]),
            device_id_type=MESH,
        )

    def ring_start(i, _):
        for side in range(2):
            first[side, i] = partial(owners[side][0], side, i)[0].astype(BF16)
            ring_copy(0, side, i).start()
        return 0

    lax.fori_loop(0, parts, ring_start, 0)

    for n in range(tiles):
        span = pl.ds(n * tile, tile)
        d_gate[:, span] = left[1, span, :].T
        d_up[:, span] = left[2, span, :].T

    def backward(n, _):
        cols = pl.ds(pl.multiple_of(n * tile, tile), tile)
        total = dot(d_gate[...], wg[:, cols]) + dot(d_up[...], wu[:, cols])
        back[:, cols] = total.astype(BF16)
        return 0

    lax.fori_loop(0, width // tile, backward, 0)

    def home_copy(i):
        k, j, q = i // (2 * YS) - far // 2, i // 2 % YS, i % 2
        return pltpu.make_async_remote_copy(
            src_ref=back.at[pl.ds(pl.multiple_of(i * cap, cap), cap), :],
            dst_ref=home_ref.at[pl.ds(pl.multiple_of(e * cap, cap), cap), :],
            send_sem=home_send.at[i],
            recv_sem=home_recv.at[e],
            device_id=(device(j, k, q), dp),
            device_id_type=MESH,
        )

    def go_home(i, _):
        home_copy(i).start()
        return 0

    lax.fori_loop(0, own, go_home, 0)
    lax.fori_loop(own + 1, sources, go_home, 0)
    kept = pltpu.make_async_copy(
        back.at[pl.ds(own * cap, cap), :],
        home_ref.at[pl.ds(pl.multiple_of(e * cap, cap), cap), :],
        w_sem.at[3],
    )
    kept.start()

    expert_lane = lax.broadcasted_iota(jnp.int32, (toks, sources), 1).astype(F32)
    names = sum(jnp.where(meta_own[:, k : k + 1] == expert_lane, 1.0, 0.0) for k in range(top))
    sooner = lax.broadcasted_iota(jnp.int32, (toks, toks), 1) < lax.broadcasted_iota(
        jnp.int32, (toks, toks), 0
    )
    place = dot(jnp.where(sooner, 1.0, 0.0).astype(BF16), names.astype(BF16))
    home_row = lax.broadcasted_iota(jnp.int32, (sources, rows), 1) // cap
    spread = home_row == lax.broadcasted_iota(jnp.int32, (sources, rows), 0)
    spread = jnp.where(spread, 1.0, 0.0).astype(BF16)
    row_lane = lax.broadcasted_iota(jnp.int32, (toks, rows), 1)
    token_map = (dot(names.astype(BF16), spread) > 0.5) & (
        dot(place.astype(BF16), spread) == (row_lane % cap).astype(F32)
    )
    row_expert = (row_lane // cap).astype(F32)

    for s in range(1, ring_size - 1):

        def ring_on(i, _):
            for side in range(2):
                ring_copy(s - 1, side, i).wait_recv()
                mine_now = partial(owners[side][s], side, i)[0]
                ring[s - 1, side, i] = (mine_now + ring[s - 1, side, i].astype(F32)).astype(BF16)
                ring_copy(s, side, i).start()
            return 0

        lax.fori_loop(0, parts, ring_on, 0)

    last = ring_size - 2

    def came_home(i, _):
        peer = (e + i) % sources
        pltpu.make_async_remote_copy(
            src_ref=back.at[pl.ds(0, cap), :],
            dst_ref=home_ref.at[pl.ds(pl.multiple_of(peer * cap, cap), cap), :],
            send_sem=home_send.at[0],
            recv_sem=home_recv.at[peer],
            device_id=(peer, dp),
            device_id_type=MESH,
        ).wait_recv()
        return 0

    kept.wait()
    lax.fori_loop(1, sources, came_home, 0)
    one_map = jnp.where(token_map, 1.0, 0.0).astype(BF16)

    def combine(n, _):
        cols = pl.ds(pl.multiple_of(n * tile, tile), tile)
        tok_out[:, cols] = dot(one_map, home_ref[:, cols]).astype(BF16)
        return 0

    lax.fori_loop(0, width // tile, combine, 0)
    unit8 = lax.broadcasted_iota(jnp.int32, (8, LANES), 0) == lax.broadcasted_iota(
        jnp.int32, (8, LANES), 1
    )
    scores = contract_last(jnp.where(unit8, 1.0, 0.0).astype(BF16), home_ref[:, width:])
    scores = scores.astype(BF16)
    which_k = lax.broadcasted_iota(jnp.int32, (top, toks), 0)
    gate_sum = jnp.zeros((top, toks), F32)
    for k in range(top):
        mine_k = token_map & (meta_own[:, k : k + 1] == row_expert)
        found = contract_last(scores, jnp.where(mine_k, 1.0, 0.0).astype(BF16))
        gate_sum = jnp.where(which_k == k, found[0:1] + found[1:2], gate_sum)
    gate_out[...] = (gate_sum / gates_ref[...].astype(F32)).astype(BF16)

    per = parts // 3
    for m, out in enumerate((down_out, gate_mat_out, up_out)):

        def ring_end(i, _):
            for side in range(2):
                ring_copy(last, side, m * per + i).wait_recv()
                total, _m, cols = partial(dp, side, m * per + i)
                sofar = ring[last, side, m * per + i].astype(F32)
                out[0, :, cols] = (total + sofar).astype(BF16)
            return 0

        lax.fori_loop(0, per, ring_end, 0)

    def left_home(i, _):
        home_copy(i).wait_send()
        return 0

    lax.fori_loop(0, own, left_home, 0)
    lax.fori_loop(own + 1, sources, left_home, 0)
    for s in range(ring_size - 1):

        def ring_sent(i, _):
            for side in range(2):
                ring_copy(s, side, i).wait_send()
            return 0

        lax.fori_loop(0, parts, ring_sent, 0)
    for copy in sends:
        copy.wait_send()


def expert_call(tokens, ids, gates, cotangent, w_gate, w_up, w_down, cap):
    toks, width = tokens.shape
    sources = lax.axis_size("expert")
    ring_size = lax.axis_size("dp")
    hid = w_gate.shape[1]
    rows = sources * cap
    tiles = hid // 256
    owned = hid // ring_size
    per = 2
    cut = width // (2 * per)
    parts = 3 * per
    far = ZS // 2
    x_copies = 5 + 3 * (YS - 1) + 1 + YS * (4 * far - 4)
    c_copies = 5 + 3 * (2 * far - 1) + 2 * far - 3 + YS * ZS
    vmem = pl.BlockSpec(memory_space=pltpu.VMEM)
    hbm = pl.BlockSpec(memory_space=pl.ANY)
    shape = jax.ShapeDtypeStruct
    dma = pltpu.SemaphoreType.DMA
    return pl.pallas_call(
        functools.partial(expert_kernel, cap),
        out_shape=(
            shape((toks, width), BF16),
            shape(gates.shape, BF16),
            shape((1, owned, width), BF16),
            shape((1, owned, width), BF16),
            shape((1, owned, width), BF16),
        ),
        in_specs=[vmem, vmem, vmem, vmem, hbm, hbm, hbm],
        out_specs=[vmem] * 5,
        scratch_shapes=[
            pltpu.VMEM((sources, toks, width + LANES), BF16),
            pltpu.VMEM((sources, toks, width), BF16),
            pltpu.VMEM((hid, width), BF16),
            pltpu.VMEM((hid, width), BF16),
            pltpu.VMEM((width, hid), BF16),
            pltpu.VMEM((hid, width), BF16),
            pltpu.VMEM((tiles, 256, rows), F32),
            pltpu.VMEM((tiles, 256, rows), F32),
            pltpu.VMEM((2, rows, width), BF16),
            pltpu.VMEM((3, hid, rows), BF16),
            pltpu.VMEM((rows, hid), BF16),
            pltpu.VMEM((rows, hid), BF16),
            pltpu.VMEM((rows, width + LANES), BF16),
            pltpu.VMEM((rows, width + LANES), BF16),
            pltpu.VMEM((2, parts, owned, cut), BF16),
            pltpu.VMEM((ring_size - 1, 2, parts, owned, cut), BF16),
            dma((x_copies,)),
            dma((sources,)),
            dma((c_copies,)),
            dma((sources,)),
            dma((sources,)),
            dma((sources,)),
            dma((ring_size - 1, 2, parts)),
            dma((ring_size - 1, 2, parts)),
            dma((4,)),
        ],
        compiler_params=pltpu.CompilerParams(
            collective_id=0, has_side_effects=True, vmem_limit_bytes=60 << 20
        ),
    )(tokens, ids, gates, cotangent, w_gate, w_up, w_down)


def body(tokens, expert_ids, gate_weights, cotangent, w_gate, w_up, w_down):
    tok_rows, top_count = expert_ids.shape
    experts = lax.axis_size("expert")
    cap = min(tok_rows, 2 * tok_rows * top_count // experts)
    token_grad, gate_grad, grad_down_t, grad_gate, grad_up = expert_call(
        tokens, expert_ids.T, gate_weights.T, cotangent, w_gate, w_up, w_down, cap
    )
    return (token_grad, gate_grad.T, grad_gate, grad_up, grad_down_t)


def solution(mesh):
    rows = P(("expert", "dp"), None)
    whole = P("expert", None, None)
    split = P("expert", "dp", None)
    return jax.shard_map(
        body,
        mesh=mesh,
        in_specs=(rows, rows, rows, rows, whole, whole, whole),
        out_specs=(rows, rows, split, split, split),
        check_vma=False,
    )
```

```python
import functools

import jax
import jax.numpy as jnp
from jax import lax
from jax.experimental import pallas as pl
from jax.experimental.pallas import tpu as pltpu
from jax.sharding import PartitionSpec as P

F32 = jnp.float32
BF16 = jnp.bfloat16
LANES = 128
MESH = pl.DeviceIdType.MESH
YS, ZS = 4, 8
GROUP = 2 * YS


def contract_last(left, right):
    return lax.dot_general(
        left, right, (((1,), (1,)), ((), ())), preferred_element_type=F32
    )


def contract_first(left, right):
    return lax.dot_general(
        left, right, (((0,), (0,)), ((), ())), preferred_element_type=F32
    )


def dot(left, right):
    return jnp.dot(left, right, preferred_element_type=F32)


def expert_kernel(
    cap,
    tok_ref,
    ids_ref,
    gates_ref,
    cot_ref,
    wg_hbm,
    wu_hbm,
    wd_hbm,
    tok_out,
    gate_out,
    down_out,
    gate_mat_out,
    up_out,
    xg,
    cg,
    wg,
    wu,
    wd,
    wd_t,
    pre_gate,
    pre_up,
    pair,
    left,
    d_gate,
    d_up,
    back,
    home_ref,
    first,
    ring,
    x_send,
    x_recv,
    c_send,
    c_recv,
    home_send,
    home_recv,
    ring_send,
    ring_recv,
    w_sem,
):
    e = lax.axis_index("expert")
    dp = lax.axis_index("dp")
    core = e % 2
    z = (e // 2) % ZS
    y = e // (2 * ZS)
    turn = 1 - 2 * core
    toks, width = tok_ref.shape
    sources = xg.shape[0]
    hid = wg.shape[0]
    rows = sources * cap
    half_rows = rows // 2
    far = ZS // 2
    group_tokens = GROUP * toks
    group_rows = GROUP * cap
    ring_size = ring.shape[0] + 1
    owned = hid // ring_size
    parts = ring.shape[2]
    cut = ring.shape[4]
    top = ids_ref.shape[0]

    loads = [
        pltpu.make_async_copy(src.at[0], dst, w_sem.at[i])
        for i, (src, dst) in enumerate(((wd_hbm, wd), (wg_hbm, wg), (wu_hbm, wu)))
    ]
    for load in loads:
        load.start()

    def device(j, k, q):
        return ((y + turn * j + YS) % YS * ZS + (z + turn * k + ZS) % ZS) * 2 + (core + q) % 2

    def spot(j, k, q=0):
        return ((k + far // 2) % ZS * YS + j % YS) * 2 + q

    hops = {
        "ahead": (device(0, 1, 0), 0, -1),
        "behind": (device(0, -1, 0), 0, 1),
        "up": (device(1, 0, 0), -1, 0),
        "down": (device(-1, 0, 0), 1, 0),
    }
    partner = device(0, 0, 1)
    ring_to = ((dp + 1) % ring_size, (dp + ring_size - 1) % ring_size)
    barrier = pltpu.get_barrier_semaphore()
    greeted = [(peer, dp) for peer in (*(hop[0] for hop in hops.values()), partner)]
    greeted += [(e, peer) for peer in ring_to]
    for peer in greeted:
        pl.semaphore_signal(barrier, inc=1, device_id=peer, device_id_type=MESH)
    named_here = jnp.concatenate([ids_ref[...].astype(F32), gates_ref[...].astype(F32)], axis=0)
    unit16 = lax.broadcasted_iota(jnp.int32, (2 * top, LANES), 0) == lax.broadcasted_iota(
        jnp.int32, (2 * top, LANES), 1
    )
    unit16 = jnp.where(unit16, 1.0, 0.0).astype(BF16)
    meta_own = contract_first(named_here.astype(BF16), unit16)
    own = spot(0, 0)
    xg[own, :, :width] = tok_ref[...]
    xg[own, :, width:] = meta_own.astype(BF16)
    cg[own] = cot_ref[...]
    pl.semaphore_wait(barrier, len(greeted))

    sends = []
    used = {"x": 0, "c": 0}

    def push(kind, j, k, ways):
        buf, ssem, rsem = (xg, x_send, x_recv) if kind == "x" else (cg, c_send, c_recv)
        for way in ways:
            if way == "partner":
                peer, there = partner, spot(-j, -k, 1)
            else:
                peer, dj, dk = hops[way]
                there = spot(j + dj, k + dk)
            copy = pltpu.make_async_remote_copy(
                src_ref=buf.at[spot(j, k)],
                dst_ref=buf.at[there],
                send_sem=ssem.at[used[kind]],
                recv_sem=rsem.at[there],
                device_id=(peer, dp),
                device_id_type=MESH,
            )
            copy.start()
            used[kind] += 1
            sends.append(copy)

    def arrived(kind, slot_at):
        buf, ssem, rsem = (xg, x_send, x_recv) if kind == "x" else (cg, c_send, c_recv)
        pltpu.make_async_remote_copy(
            src_ref=buf.at[slot_at],
            dst_ref=buf.at[slot_at],
            send_sem=ssem.at[0],
            recv_sem=rsem.at[slot_at],
            device_id=(partner, dp),
            device_id_type=MESH,
        ).wait_recv()

    def along_z(k):
        if -far < k < 0:
            return ["ahead"]
        return ["behind"] if 0 < k < far - 1 else []

    def x_step(j, k):
        arrived("x", spot(j, k))
        ways = ["ahead", "behind"] if k == 0 else along_z(k)
        if k == 0 and j == -1:
            ways = ["up", *ways]
        push("x", j, k, [*ways, "partner"])

    def c_step(k):
        arrived("c", spot(0, k))
        push("c", 0, k, [*along_z(k), "up", "down", "partner"])

    def c_hand(j, k):
        arrived("c", spot(j, k))
        push("c", j, k, ["up", "partner"] if j == -1 else ["partner"])

    before = lax.broadcasted_iota(jnp.int32, (group_tokens, group_tokens), 0)
    after = lax.broadcasted_iota(jnp.int32, (group_tokens, group_tokens), 1)
    earlier = ((before < after) & (before // toks == after // toks)).astype(F32).astype(BF16)
    row = lax.broadcasted_iota(jnp.int32, (group_rows, group_tokens), 0)
    col = lax.broadcasted_iota(jnp.int32, (group_rows, group_tokens), 1)
    own_block = row // cap == col // toks
    slot = (row % cap).astype(F32)
    lane = lax.broadcasted_iota(jnp.int32, (group_tokens, LANES), 1)
    mine = e.astype(F32)
    ones = jnp.ones((8, LANES), BF16)
    tile = 256
    tiles = hid // tile

    def select(g):
        block = pl.ds(g * GROUP, GROUP)
        meta = xg[block, :, width:].reshape(group_tokens, LANES).astype(F32)
        named = (meta == mine) & (lane < top)
        gate = jnp.where(named, pltpu.roll(meta, LANES - top, 1), 0.0).astype(BF16)
        hits = jnp.where(named, 1.0, 0.0).astype(BF16)
        here = contract_last(ones, hits)
        rank = dot(here.astype(BF16), earlier)
        weight = contract_last(ones, gate)[0:1]
        chosen = own_block & (here[0:1] > 0.5) & (rank[0:1] == slot)
        return chosen, weight

    def handed(kind, half):
        for k in range(-(far // 2), far // 2):
            for j in range(YS):
                arrived(kind, spot(j, k + half * far, 1))

    def take_x(half):
        handed("x", half)
        base = half * half_rows

        def pick(j, _):
            g = half * (sources // GROUP // 2) + j
            chosen, _w = select(g)
            tokens = xg[pl.ds(g * GROUP, GROUP), :, :width].reshape(group_tokens, width)
            one_hot = jnp.where(chosen, 1.0, 0.0).astype(BF16)
            start = pl.multiple_of(base + j * group_rows, group_rows)
            pair[0, pl.ds(start, group_rows), :] = dot(one_hot, tokens).astype(BF16)
            return 0

        lax.fori_loop(0, sources // GROUP // 2, pick, 0)
        span = pl.ds(base, half_rows)

        def forward(n, _):
            cols = pl.ds(pl.multiple_of(n * tile, tile), tile)
            pre_gate[n, :, span] = contract_last(wg[cols, :], pair[0, span, :])
            pre_up[n, :, span] = contract_last(wu[cols, :], pair[0, span, :])
            return 0

        lax.fori_loop(0, tiles, forward, 0)

    def take_c(half):
        handed("c", half)
        base = half * half_rows

        def pick(j, _):
            g = half * (sources // GROUP // 2) + j
            chosen, weight = select(g)
            cots = cg[pl.ds(g * GROUP, GROUP)].reshape(group_tokens, width)
            one_gate = jnp.where(chosen, weight, 0.0).astype(BF16)
            start = pl.multiple_of(base + j * group_rows, group_rows)
            pair[1, pl.ds(start, group_rows), :] = dot(one_gate, cots).astype(BF16)
            return 0

        lax.fori_loop(0, sources // GROUP // 2, pick, 0)
        span = pl.ds(base, half_rows)

        def grads(n, score):
            cols = pl.ds(pl.multiple_of(n * tile, tile), tile)
            d_hidden = contract_last(wd_t[cols, :], pair[1, span, :])
            gate, up = pre_gate[n, :, span], pre_up[n, :, span]
            sig = jax.nn.sigmoid(gate)
            act = gate * sig
            hidden = (act * up).astype(BF16)
            left[0, cols, span] = hidden
            left[1, cols, span] = (
                d_hidden * up * sig * (1.0 + gate * (1.0 - sig))
            ).astype(BF16)
            left[2, cols, span] = (d_hidden * act).astype(BF16)
            return score + jnp.sum(hidden.astype(F32) * d_hidden, axis=0, keepdims=True)

        score = lax.fori_loop(0, tiles, grads, jnp.zeros((1, half_rows), F32))
        high = score.astype(BF16).astype(F32)
        which = lax.broadcasted_iota(jnp.int32, (8, half_rows), 0)
        both = jnp.where(which == 0, high, jnp.where(which == 1, score - high, 0.0))
        unit = lax.broadcasted_iota(jnp.int32, (8, LANES), 0) == lax.broadcasted_iota(
            jnp.int32, (8, LANES), 1
        )
        unit = jnp.where(unit, 1.0, 0.0).astype(BF16)
        back[span, width:] = contract_first(both.astype(BF16), unit).astype(BF16)

    def turn_down(c):
        span = pl.ds(c * tile, tile)
        wd_t[:, span] = wd[span, :].T

    push("x", 0, 0, ["up", "down", "ahead", "behind"])
    push("c", 0, 0, ["ahead", "behind", "up", "down"])
    push("x", 0, 0, ["partner"])
    push("c", 0, 0, ["partner"])
    turns = list(range(width // tile))
    loads[0].wait()
    turn_down(turns.pop())
    for j in (-1, 1, -2):
        x_step(j, 0)

    def both_ways(k):
        return (0,) if k == 0 else (-k, k) if k < far else (-k,)

    def c_turn(at):
        for k in range(far + 1):
            if k > 0 and at == k + 1:
                for way in both_ways(k):
                    c_step(way)
            if at == k + 3:
                for way in both_ways(k):
                    c_hand(-1, way)
                    c_hand(1, way)
            if at == k + 4:
                for way in both_ways(k):
                    c_hand(-2, way)

    for k in range(1, far + 1):
        for h, js in enumerate(((0, -1), (1, -2))):
            c_turn(2 * k + h)
            for j in js:
                for way in both_ways(k):
                    x_step(j, way)
                if turns:
                    turn_down(turns.pop())
        if k == far // 2:
            loads[1].wait()
            loads[2].wait()
            take_x(0)
        if k < far and 2 * k + 1 >= far // 2 + 4:
            while turns:
                turn_down(turns.pop())
            take_c(0)
    for at in range(2 * far + 2, far + 5):
        c_turn(at)
    while turns:
        turn_down(turns.pop())
    take_x(1)
    if 2 * far - 1 < far // 2 + 4:
        take_c(0)
    take_c(1)

    owners = [
        [(dp + ring_size - 1 - s) % ring_size for s in range(ring_size)],
        [(dp + 1 + s) % ring_size for s in range(ring_size)],
    ]

    def partial(owner, side, i):
        per = parts // 3
        m = i // per
        cols = pl.ds(pl.multiple_of((side * per + i % per) * cut, cut), cut)
        lhs = left[m, pl.ds(pl.multiple_of(owner * owned, 16), owned), :]
        return dot(lhs, pair[(3 - m) // 3, :, cols]), m, cols

    def ring_copy(s, side, i):
        return pltpu.make_async_remote_copy(
            src_ref=first.at[side, i] if s == 0 else ring.at[s - 1, side, i],
            dst_ref=ring.at[s, side, i],
            send_sem=ring_send.at[s, side, i],
            recv_sem=ring_recv.at[s, side, i],
            device_id=(e, ring_to[side]),
            device_id_type=MESH,
        )

    def ring_start(i, _):
        for side in range(2):
            first[side, i] = partial(owners[side][0], side, i)[0].astype(BF16)
            ring_copy(0, side, i).start()
        return 0

    lax.fori_loop(0, parts, ring_start, 0)

    for n in range(tiles):
        span = pl.ds(n * tile, tile)
        d_gate[:, span] = left[1, span, :].T
        d_up[:, span] = left[2, span, :].T

    def backward(n, _):
        cols = pl.ds(pl.multiple_of(n * tile, tile), tile)
        total = dot(d_gate[...], wg[:, cols]) + dot(d_up[...], wu[:, cols])
        back[:, cols] = total.astype(BF16)
        return 0

    lax.fori_loop(0, width // tile, backward, 0)

    def home_copy(i):
        k, j, q = i // (2 * YS) - far // 2, i // 2 % YS, i % 2
        return pltpu.make_async_remote_copy(
            src_ref=back.at[pl.ds(pl.multiple_of(i * cap, cap), cap), :],
            dst_ref=home_ref.at[pl.ds(pl.multiple_of(e * cap, cap), cap), :],
            send_sem=home_send.at[i],
            recv_sem=home_recv.at[e],
            device_id=(device(j, k, q), dp),
            device_id_type=MESH,
        )

    def go_home(i, _):
        home_copy(i).start()
        return 0

    lax.fori_loop(0, own, go_home, 0)
    lax.fori_loop(own + 1, sources, go_home, 0)
    kept = pltpu.make_async_copy(
        back.at[pl.ds(own * cap, cap), :],
        home_ref.at[pl.ds(pl.multiple_of(e * cap, cap), cap), :],
        w_sem.at[3],
    )
    kept.start()

    expert_lane = lax.broadcasted_iota(jnp.int32, (toks, sources), 1).astype(F32)
    names = sum(jnp.where(meta_own[:, k : k + 1] == expert_lane, 1.0, 0.0) for k in range(top))
    sooner = lax.broadcasted_iota(jnp.int32, (toks, toks), 1) < lax.broadcasted_iota(
        jnp.int32, (toks, toks), 0
    )
    place = dot(jnp.where(sooner, 1.0, 0.0).astype(BF16), names.astype(BF16))
    home_row = lax.broadcasted_iota(jnp.int32, (sources, rows), 1) // cap
    spread = home_row == lax.broadcasted_iota(jnp.int32, (sources, rows), 0)
    spread = jnp.where(spread, 1.0, 0.0).astype(BF16)
    row_lane = lax.broadcasted_iota(jnp.int32, (toks, rows), 1)
    token_map = (dot(names.astype(BF16), spread) > 0.5) & (
        dot(place.astype(BF16), spread) == (row_lane % cap).astype(F32)
    )
    row_expert = (row_lane // cap).astype(F32)

    for s in range(1, ring_size - 1):

        def ring_on(i, _):
            for side in range(2):
                ring_copy(s - 1, side, i).wait_recv()
                mine_now = partial(owners[side][s], side, i)[0]
                ring[s - 1, side, i] = (mine_now + ring[s - 1, side, i].astype(F32)).astype(BF16)
                ring_copy(s, side, i).start()
            return 0

        lax.fori_loop(0, parts, ring_on, 0)

    last = ring_size - 2

    def came_home(i, _):
        peer = (e + i) % sources
        pltpu.make_async_remote_copy(
            src_ref=back.at[pl.ds(0, cap), :],
            dst_ref=home_ref.at[pl.ds(pl.multiple_of(peer * cap, cap), cap), :],
            send_sem=home_send.at[0],
            recv_sem=home_recv.at[peer],
            device_id=(peer, dp),
            device_id_type=MESH,
        ).wait_recv()
        return 0

    kept.wait()
    lax.fori_loop(1, sources, came_home, 0)
    one_map = jnp.where(token_map, 1.0, 0.0).astype(BF16)

    def combine(n, _):
        cols = pl.ds(pl.multiple_of(n * tile, tile), tile)
        tok_out[:, cols] = dot(one_map, home_ref[:, cols]).astype(BF16)
        return 0

    lax.fori_loop(0, width // tile, combine, 0)
    unit8 = lax.broadcasted_iota(jnp.int32, (8, LANES), 0) == lax.broadcasted_iota(
        jnp.int32, (8, LANES), 1
    )
    scores = contract_last(jnp.where(unit8, 1.0, 0.0).astype(BF16), home_ref[:, width:])
    scores = scores.astype(BF16)
    which_k = lax.broadcasted_iota(jnp.int32, (top, toks), 0)
    gate_sum = jnp.zeros((top, toks), F32)
    for k in range(top):
        mine_k = token_map & (meta_own[:, k : k + 1] == row_expert)
        found = contract_last(scores, jnp.where(mine_k, 1.0, 0.0).astype(BF16))
        gate_sum = jnp.where(which_k == k, found[0:1] + found[1:2], gate_sum)
    gate_out[...] = (gate_sum / gates_ref[...].astype(F32)).astype(BF16)

    per = parts // 3
    for m, out in enumerate((down_out, gate_mat_out, up_out)):

        def ring_end(i, _):
            for side in range(2):
                ring_copy(last, side, m * per + i).wait_recv()
                total, _m, cols = partial(dp, side, m * per + i)
                sofar = ring[last, side, m * per + i].astype(F32)
                out[0, :, cols] = (total + sofar).astype(BF16)
            return 0

        lax.fori_loop(0, per, ring_end, 0)

    def left_home(i, _):
        home_copy(i).wait_send()
        return 0

    lax.fori_loop(0, own, left_home, 0)
    lax.fori_loop(own + 1, sources, left_home, 0)
    for s in range(ring_size - 1):

        def ring_sent(i, _):
            for side in range(2):
                ring_copy(s, side, i).wait_send()
            return 0

        lax.fori_loop(0, parts, ring_sent, 0)
    for copy in sends:
        copy.wait_send()


def expert_call(tokens, ids, gates, cotangent, w_gate, w_up, w_down, cap):
    toks, width = tokens.shape
    sources = lax.axis_size("expert")
    ring_size = lax.axis_size("dp")
    hid = w_gate.shape[1]
    rows = sources * cap
    tiles = hid // 256
    owned = hid // ring_size
    per = 2
    cut = width // (2 * per)
    parts = 3 * per
    far = ZS // 2
    x_copies = 5 + 3 * (YS - 1) + 1 + YS * (4 * far - 4)
    c_copies = 5 + 3 * (2 * far - 1) + 2 * far - 3 + YS * ZS
    vmem = pl.BlockSpec(memory_space=pltpu.VMEM)
    hbm = pl.BlockSpec(memory_space=pl.ANY)
    shape = jax.ShapeDtypeStruct
    dma = pltpu.SemaphoreType.DMA
    return pl.pallas_call(
        functools.partial(expert_kernel, cap),
        out_shape=(
            shape((toks, width), BF16),
            shape(gates.shape, BF16),
            shape((1, owned, width), BF16),
            shape((1, owned, width), BF16),
            shape((1, owned, width), BF16),
        ),
        in_specs=[vmem, vmem, vmem, vmem, hbm, hbm, hbm],
        out_specs=[vmem] * 5,
        scratch_shapes=[
            pltpu.VMEM((sources, toks, width + LANES), BF16),
            pltpu.VMEM((sources, toks, width), BF16),
            pltpu.VMEM((hid, width), BF16),
            pltpu.VMEM((hid, width), BF16),
            pltpu.VMEM((width, hid), BF16),
            pltpu.VMEM((hid, width), BF16),
            pltpu.VMEM((tiles, 256, rows), F32),
            pltpu.VMEM((tiles, 256, rows), F32),
            pltpu.VMEM((2, rows, width), BF16),
            pltpu.VMEM((3, hid, rows), BF16),
            pltpu.VMEM((rows, hid), BF16),
            pltpu.VMEM((rows, hid), BF16),
            pltpu.VMEM((rows, width + LANES), BF16),
            pltpu.VMEM((rows, width + LANES), BF16),
            pltpu.VMEM((2, parts, owned, cut), BF16),
            pltpu.VMEM((ring_size - 1, 2, parts, owned, cut), BF16),
            dma((x_copies,)),
            dma((sources,)),
            dma((c_copies,)),
            dma((sources,)),
            dma((sources,)),
            dma((sources,)),
            dma((ring_size - 1, 2, parts)),
            dma((ring_size - 1, 2, parts)),
            dma((4,)),
        ],
        compiler_params=pltpu.CompilerParams(
            collective_id=0, has_side_effects=True, vmem_limit_bytes=60 << 20
        ),
    )(tokens, ids, gates, cotangent, w_gate, w_up, w_down)


def settle_kernel(count, *refs):
    for i in range(count):
        refs[count + i][...] = refs[i][...]


def settle(*arrays):
    count = len(arrays)
    vmem = pl.BlockSpec(memory_space=pltpu.VMEM)
    return pl.pallas_call(
        functools.partial(settle_kernel, count),
        out_shape=tuple(jax.ShapeDtypeStruct(a.shape, a.dtype) for a in arrays),
        in_specs=[vmem] * count,
        out_specs=[vmem] * count,
        compiler_params=pltpu.CompilerParams(vmem_limit_bytes=16 << 20),
    )(*arrays)


def body(tokens, expert_ids, gate_weights, cotangent, w_gate, w_up, w_down):
    tok_rows, top_count = expert_ids.shape
    experts = lax.axis_size("expert")
    cap = min(tok_rows, 2 * tok_rows * top_count // experts)
    token_grad, gate_grad, grad_down_t, grad_gate, grad_up = expert_call(
        tokens, expert_ids.T, gate_weights.T, cotangent, w_gate, w_up, w_down, cap
    )
    token_grad, gate_grad, grad_gate, grad_up, grad_down_t = settle(
        token_grad, gate_grad, grad_gate, grad_up, grad_down_t
    )
    return (token_grad, gate_grad.T, grad_gate, grad_up, grad_down_t)


def solution(mesh):
    rows = P(("expert", "dp"), None)
    whole = P("expert", None, None)
    split = P("expert", "dp", None)
    return jax.shard_map(
        body,
        mesh=mesh,
        in_specs=(rows, rows, rows, rows, whole, whole, whole),
        out_specs=(rows, rows, split, split, split),
        check_vma=False,
    )
```

```python
import functools

import jax
import jax.numpy as jnp
from jax import lax
from jax.experimental import pallas as pl
from jax.experimental.pallas import tpu as pltpu
from jax.sharding import PartitionSpec as P

F32 = jnp.float32
BF16 = jnp.bfloat16
LANES = 128
MESH = pl.DeviceIdType.MESH
YS, ZS = 4, 8
GROUP = 2 * YS


def contract_last(left, right):
    return lax.dot_general(
        left, right, (((1,), (1,)), ((), ())), preferred_element_type=F32
    )


def contract_first(left, right):
    return lax.dot_general(
        left, right, (((0,), (0,)), ((), ())), preferred_element_type=F32
    )


def dot(left, right):
    return jnp.dot(left, right, preferred_element_type=F32)


def expert_kernel(
    cap,
    tok_ref,
    ids_ref,
    gates_ref,
    cot_ref,
    wg_hbm,
    wu_hbm,
    wd_hbm,
    tok_out,
    gate_out,
    down_out,
    gate_mat_out,
    up_out,
    xg,
    cg,
    wg,
    wu,
    wd,
    wd_t,
    pre_gate,
    pre_up,
    pair,
    gate_hot,
    left,
    d_gate,
    d_up,
    back,
    home_ref,
    first,
    ring,
    x_send,
    x_recv,
    c_send,
    c_recv,
    home_send,
    home_recv,
    ring_send,
    ring_recv,
    out_sem,
    w_sem,
):
    e = lax.axis_index("expert")
    dp = lax.axis_index("dp")
    core = e % 2
    z = (e // 2) % ZS
    y = e // (2 * ZS)
    turn = 1 - 2 * core
    toks, width = tok_ref.shape
    sources = xg.shape[0]
    hid = wg.shape[0]
    rows = sources * cap
    half_rows = rows // 2
    far = ZS // 2
    group_tokens = GROUP * toks
    group_rows = GROUP * cap
    ring_size = ring.shape[0] + 1
    owned = hid // ring_size
    parts = ring.shape[2]
    cut = ring.shape[4]
    top = ids_ref.shape[0]

    loads = [
        pltpu.make_async_copy(src.at[0], dst, w_sem.at[i])
        for i, (src, dst) in enumerate(((wd_hbm, wd), (wg_hbm, wg), (wu_hbm, wu)))
    ]
    for load in loads:
        load.start()

    def device(j, k, q):
        return ((y + turn * j + YS) % YS * ZS + (z + turn * k + ZS) % ZS) * 2 + (core + q) % 2

    def spot(j, k, q=0):
        return ((k + far // 2) % ZS * YS + j % YS) * 2 + q

    hops = {
        "ahead": (device(0, 1, 0), 0, -1),
        "behind": (device(0, -1, 0), 0, 1),
        "up": (device(1, 0, 0), -1, 0),
        "down": (device(-1, 0, 0), 1, 0),
    }
    partner = device(0, 0, 1)
    ring_to = ((dp + 1) % ring_size, (dp + ring_size - 1) % ring_size)
    barrier = pltpu.get_barrier_semaphore()
    greeted = [(peer, dp) for peer in (*(hop[0] for hop in hops.values()), partner)]
    greeted += [(e, peer) for peer in ring_to]
    for peer in greeted:
        pl.semaphore_signal(barrier, inc=1, device_id=peer, device_id_type=MESH)
    named_here = jnp.concatenate([ids_ref[...].astype(F32), gates_ref[...].astype(F32)], axis=0)
    unit16 = lax.broadcasted_iota(jnp.int32, (2 * top, LANES), 0) == lax.broadcasted_iota(
        jnp.int32, (2 * top, LANES), 1
    )
    unit16 = jnp.where(unit16, 1.0, 0.0).astype(BF16)
    meta_own = contract_first(named_here.astype(BF16), unit16)
    own = spot(0, 0)
    xg[own, :, :width] = tok_ref[...]
    xg[own, :, width:] = meta_own.astype(BF16)
    cg[own] = cot_ref[...]
    pl.semaphore_wait(barrier, len(greeted))

    sends = []
    used = {"x": 0, "c": 0}

    def push(kind, j, k, ways):
        buf, ssem, rsem = (xg, x_send, x_recv) if kind == "x" else (cg, c_send, c_recv)
        for way in ways:
            if way == "partner":
                peer, there = partner, spot(-j, -k, 1)
            else:
                peer, dj, dk = hops[way]
                there = spot(j + dj, k + dk)
            copy = pltpu.make_async_remote_copy(
                src_ref=buf.at[spot(j, k)],
                dst_ref=buf.at[there],
                send_sem=ssem.at[used[kind]],
                recv_sem=rsem.at[there],
                device_id=(peer, dp),
                device_id_type=MESH,
            )
            copy.start()
            used[kind] += 1
            sends.append(copy)

    def arrived(kind, slot_at):
        buf, ssem, rsem = (xg, x_send, x_recv) if kind == "x" else (cg, c_send, c_recv)
        pltpu.make_async_remote_copy(
            src_ref=buf.at[slot_at],
            dst_ref=buf.at[slot_at],
            send_sem=ssem.at[0],
            recv_sem=rsem.at[slot_at],
            device_id=(partner, dp),
            device_id_type=MESH,
        ).wait_recv()

    def along_z(k):
        if -far < k < 0:
            return ["ahead"]
        return ["behind"] if 0 < k < far - 1 else []

    def x_step(j, k):
        arrived("x", spot(j, k))
        ways = ["ahead", "behind"] if k == 0 else along_z(k)
        if k == 0 and j == -1:
            ways = ["up", *ways]
        push("x", j, k, [*ways, "partner"])

    def c_step(k):
        arrived("c", spot(0, k))
        push("c", 0, k, [*along_z(k), "up", "down", "partner"])

    def c_hand(j, k):
        arrived("c", spot(j, k))
        push("c", j, k, ["up", "partner"] if j == -1 else ["partner"])

    before = lax.broadcasted_iota(jnp.int32, (group_tokens, group_tokens), 0)
    after = lax.broadcasted_iota(jnp.int32, (group_tokens, group_tokens), 1)
    earlier = ((before < after) & (before // toks == after // toks)).astype(F32).astype(BF16)
    row = lax.broadcasted_iota(jnp.int32, (group_rows, group_tokens), 0)
    col = lax.broadcasted_iota(jnp.int32, (group_rows, group_tokens), 1)
    own_block = row // cap == col // toks
    slot = (row % cap).astype(F32)
    lane = lax.broadcasted_iota(jnp.int32, (group_tokens, LANES), 1)
    mine = e.astype(F32)
    ones = jnp.ones((8, LANES), BF16)
    tile = 256
    tiles = hid // tile

    def select(g):
        block = pl.ds(g * GROUP, GROUP)
        meta = xg[block, :, width:].reshape(group_tokens, LANES).astype(F32)
        named = (meta == mine) & (lane < top)
        gate = jnp.where(named, pltpu.roll(meta, LANES - top, 1), 0.0).astype(BF16)
        hits = jnp.where(named, 1.0, 0.0).astype(BF16)
        here = contract_last(ones, hits)
        rank = dot(here.astype(BF16), earlier)
        weight = contract_last(ones, gate)[0:1]
        chosen = own_block & (here[0:1] > 0.5) & (rank[0:1] == slot)
        return chosen, weight

    def handed(kind, p):
        for j in range(YS):
            arrived(kind, spot(j, p - far // 2, 1))

    def pick_x(p):
        handed("x", p)
        chosen, weight = select(p)
        tokens = xg[p * GROUP : (p + 1) * GROUP, :, :width].reshape(group_tokens, width)
        one_hot = jnp.where(chosen, 1.0, 0.0).astype(BF16)
        gate_hot[p] = jnp.where(chosen, weight, 0.0).astype(BF16)
        span = pl.ds(p * group_rows, group_rows)
        pair[0, span, :] = dot(one_hot, tokens).astype(BF16)

    def pick_c(p):
        handed("c", p)
        cots = cg[p * GROUP : (p + 1) * GROUP].reshape(group_tokens, width)
        span = pl.ds(p * group_rows, group_rows)
        pair[1, span, :] = dot(gate_hot[p], cots).astype(BF16)

    def take_x(half):
        span = pl.ds(half * half_rows, half_rows)

        def forward(n, _):
            cols = pl.ds(pl.multiple_of(n * tile, tile), tile)
            pre_gate[n, :, span] = contract_last(wg[cols, :], pair[0, span, :])
            pre_up[n, :, span] = contract_last(wu[cols, :], pair[0, span, :])
            return 0

        lax.fori_loop(0, tiles, forward, 0)

    def take_c(half):
        span = pl.ds(half * half_rows, half_rows)

        def grads(n, score):
            cols = pl.ds(pl.multiple_of(n * tile, tile), tile)
            d_hidden = contract_last(wd_t[cols, :], pair[1, span, :])
            gate, up = pre_gate[n, :, span], pre_up[n, :, span]
            sig = jax.nn.sigmoid(gate)
            act = gate * sig
            hidden = (act * up).astype(BF16)
            left[0, cols, span] = hidden
            left[1, cols, span] = (
                d_hidden * up * sig * (1.0 + gate * (1.0 - sig))
            ).astype(BF16)
            left[2, cols, span] = (d_hidden * act).astype(BF16)
            return score + jnp.sum(hidden.astype(F32) * d_hidden, axis=0, keepdims=True)

        score = lax.fori_loop(0, tiles, grads, jnp.zeros((1, half_rows), F32))
        high = score.astype(BF16).astype(F32)
        which = lax.broadcasted_iota(jnp.int32, (8, half_rows), 0)
        both = jnp.where(which == 0, high, jnp.where(which == 1, score - high, 0.0))
        unit = lax.broadcasted_iota(jnp.int32, (8, LANES), 0) == lax.broadcasted_iota(
            jnp.int32, (8, LANES), 1
        )
        unit = jnp.where(unit, 1.0, 0.0).astype(BF16)
        back[span, width:] = contract_first(both.astype(BF16), unit).astype(BF16)

    def turn_down(c):
        span = pl.ds(c * tile, tile)
        wd_t[:, span] = wd[span, :].T

    push("x", 0, 0, ["up", "down", "ahead", "behind"])
    push("c", 0, 0, ["ahead", "behind", "up", "down"])
    push("x", 0, 0, ["partner"])
    push("c", 0, 0, ["partner"])
    turns = list(range(width // tile))
    for j in (-1, 1, -2):
        x_step(j, 0)

    def both_ways(k):
        return (0,) if k == 0 else (-k, k) if k < far else (-k,)

    def c_turn(at):
        for k in range(far + 1):
            if k > 0 and at == k + 1:
                for way in both_ways(k):
                    c_step(way)
            if at == k + 3:
                for way in both_ways(k):
                    c_hand(-1, way)
                    c_hand(1, way)
            if at == k + 4:
                for way in both_ways(k):
                    c_hand(-2, way)

    for k in range(1, far + 1):
        for h, js in enumerate(((0, -1), (1, -2))):
            c_turn(2 * k + h)
            if k == far - 1 and h == 0:
                for p in (1, 2, 3):
                    pick_c(p)
            for j in js:
                for way in both_ways(k):
                    x_step(j, way)
                if turns and k > 1:
                    turn_down(turns.pop())
        if k == 1:
            for load in loads:
                load.wait()
            for p in (1, 2, 3):
                pick_x(p)
        if k == 2:
            pick_x(0)
            pick_x(4)
            take_x(0)
        if k == far - 1:
            while turns:
                turn_down(turns.pop())
            pick_c(0)
            pick_c(4)
            take_c(0)
            pick_x(5)
            pick_x(7)
    pick_c(5)
    pick_c(7)
    pick_x(6)
    take_x(1)
    pick_c(6)
    take_c(1)

    owners = [
        [(dp + ring_size - 1 - s) % ring_size for s in range(ring_size)],
        [(dp + 1 + s) % ring_size for s in range(ring_size)],
    ]

    def partial(owner, side, i):
        per = parts // 3
        m = i // per
        cols = pl.ds(pl.multiple_of((side * per + i % per) * cut, cut), cut)
        lhs = left[m, pl.ds(pl.multiple_of(owner * owned, 16), owned), :]
        return dot(lhs, pair[(3 - m) // 3, :, cols]), m, cols

    def ring_copy(s, side, i):
        return pltpu.make_async_remote_copy(
            src_ref=first.at[side, i] if s == 0 else ring.at[s - 1, side, i],
            dst_ref=ring.at[s, side, i],
            send_sem=ring_send.at[s, side, i],
            recv_sem=ring_recv.at[s, side, i],
            device_id=(e, ring_to[side]),
            device_id_type=MESH,
        )

    def ring_start(i, _):
        for side in range(2):
            first[side, i] = partial(owners[side][0], side, i)[0].astype(BF16)
            ring_copy(0, side, i).start()
        return 0

    lax.fori_loop(0, parts, ring_start, 0)

    for n in range(tiles):
        span = pl.ds(n * tile, tile)
        d_gate[:, span] = left[1, span, :].T
        d_up[:, span] = left[2, span, :].T

    def backward(n, _):
        cols = pl.ds(pl.multiple_of(n * tile, tile), tile)
        total = dot(d_gate[...], wg[:, cols]) + dot(d_up[...], wu[:, cols])
        back[:, cols] = total.astype(BF16)
        return 0

    lax.fori_loop(0, width // tile, backward, 0)

    def home_copy(i):
        k, j, q = i // (2 * YS) - far // 2, i // 2 % YS, i % 2
        return pltpu.make_async_remote_copy(
            src_ref=back.at[pl.ds(pl.multiple_of(i * cap, cap), cap), :],
            dst_ref=home_ref.at[pl.ds(pl.multiple_of(e * cap, cap), cap), :],
            send_sem=home_send.at[i],
            recv_sem=home_recv.at[e],
            device_id=(device(j, k, q), dp),
            device_id_type=MESH,
        )

    def go_home(i, _):
        home_copy(i).start()
        return 0

    lax.fori_loop(0, own, go_home, 0)
    lax.fori_loop(own + 1, sources, go_home, 0)
    kept = pltpu.make_async_copy(
        back.at[pl.ds(own * cap, cap), :],
        home_ref.at[pl.ds(pl.multiple_of(e * cap, cap), cap), :],
        w_sem.at[3],
    )
    kept.start()

    expert_lane = lax.broadcasted_iota(jnp.int32, (toks, sources), 1).astype(F32)
    names = sum(jnp.where(meta_own[:, k : k + 1] == expert_lane, 1.0, 0.0) for k in range(top))
    sooner = lax.broadcasted_iota(jnp.int32, (toks, toks), 1) < lax.broadcasted_iota(
        jnp.int32, (toks, toks), 0
    )
    place = dot(jnp.where(sooner, 1.0, 0.0).astype(BF16), names.astype(BF16))
    home_row = lax.broadcasted_iota(jnp.int32, (sources, rows), 1) // cap
    spread = home_row == lax.broadcasted_iota(jnp.int32, (sources, rows), 0)
    spread = jnp.where(spread, 1.0, 0.0).astype(BF16)
    row_lane = lax.broadcasted_iota(jnp.int32, (toks, rows), 1)
    token_map = (dot(names.astype(BF16), spread) > 0.5) & (
        dot(place.astype(BF16), spread) == (row_lane % cap).astype(F32)
    )
    row_expert = (row_lane // cap).astype(F32)

    for s in range(1, ring_size - 1):

        def ring_on(i, _):
            for side in range(2):
                ring_copy(s - 1, side, i).wait_recv()
                mine_now = partial(owners[side][s], side, i)[0]
                ring[s - 1, side, i] = (mine_now + ring[s - 1, side, i].astype(F32)).astype(BF16)
                ring_copy(s, side, i).start()
            return 0

        lax.fori_loop(0, parts, ring_on, 0)

    last = ring_size - 2

    def came_home(i, _):
        peer = (e + i) % sources
        pltpu.make_async_remote_copy(
            src_ref=back.at[pl.ds(0, cap), :],
            dst_ref=home_ref.at[pl.ds(pl.multiple_of(peer * cap, cap), cap), :],
            send_sem=home_send.at[0],
            recv_sem=home_recv.at[peer],
            device_id=(peer, dp),
            device_id_type=MESH,
        ).wait_recv()
        return 0

    kept.wait()
    lax.fori_loop(1, sources, came_home, 0)
    one_map = jnp.where(token_map, 1.0, 0.0).astype(BF16)

    def combine(n, _):
        cols = pl.ds(pl.multiple_of(n * tile, tile), tile)
        tok_out[:, cols] = dot(one_map, home_ref[:, cols]).astype(BF16)
        return 0

    lax.fori_loop(0, width // tile, combine, 0)
    unit8 = lax.broadcasted_iota(jnp.int32, (8, LANES), 0) == lax.broadcasted_iota(
        jnp.int32, (8, LANES), 1
    )
    scores = contract_last(jnp.where(unit8, 1.0, 0.0).astype(BF16), home_ref[:, width:])
    scores = scores.astype(BF16)
    which_k = lax.broadcasted_iota(jnp.int32, (top, toks), 0)
    gate_sum = jnp.zeros((top, toks), F32)
    for k in range(top):
        mine_k = token_map & (meta_own[:, k : k + 1] == row_expert)
        found = contract_last(scores, jnp.where(mine_k, 1.0, 0.0).astype(BF16))
        gate_sum = jnp.where(which_k == k, found[0:1] + found[1:2], gate_sum)
    gate_out[...] = (gate_sum / gates_ref[...].astype(F32)).astype(BF16)

    per = parts // 3

    def out_copy(out, side, i, cols):
        return pltpu.make_async_copy(
            ring.at[last, side, i], out.at[0, :, cols], out_sem.at[side, i]
        )

    for m, out in enumerate((down_out, gate_mat_out, up_out)):

        def ring_end(i, _):
            for side in range(2):
                ring_copy(last, side, m * per + i).wait_recv()
                total, _m, cols = partial(dp, side, m * per + i)
                sofar = ring[last, side, m * per + i].astype(F32)
                ring[last, side, m * per + i] = (total + sofar).astype(BF16)
                out_copy(out, side, m * per + i, cols).start()
            return 0

        lax.fori_loop(0, per, ring_end, 0)

    for m, out in enumerate((down_out, gate_mat_out, up_out)):

        def out_done(i, _):
            for side in range(2):
                cols = pl.ds(pl.multiple_of((side * per + i) * cut, cut), cut)
                out_copy(out, side, m * per + i, cols).wait()
            return 0

        lax.fori_loop(0, per, out_done, 0)

    def left_home(i, _):
        home_copy(i).wait_send()
        return 0

    lax.fori_loop(0, own, left_home, 0)
    lax.fori_loop(own + 1, sources, left_home, 0)
    for s in range(ring_size - 1):

        def ring_sent(i, _):
            for side in range(2):
                ring_copy(s, side, i).wait_send()
            return 0

        lax.fori_loop(0, parts, ring_sent, 0)
    for copy in sends:
        copy.wait_send()


def expert_call(tokens, ids, gates, cotangent, w_gate, w_up, w_down, cap):
    toks, width = tokens.shape
    sources = lax.axis_size("expert")
    ring_size = lax.axis_size("dp")
    hid = w_gate.shape[1]
    rows = sources * cap
    tiles = hid // 256
    owned = hid // ring_size
    per = 2
    cut = width // (2 * per)
    parts = 3 * per
    far = ZS // 2
    x_copies = 5 + 3 * (YS - 1) + 1 + YS * (4 * far - 4)
    c_copies = 5 + 3 * (2 * far - 1) + 2 * far - 3 + YS * ZS
    vmem = pl.BlockSpec(memory_space=pltpu.VMEM)
    hbm = pl.BlockSpec(memory_space=pl.ANY)
    shape = jax.ShapeDtypeStruct
    dma = pltpu.SemaphoreType.DMA
    return pl.pallas_call(
        functools.partial(expert_kernel, cap),
        out_shape=(
            shape((toks, width), BF16),
            shape(gates.shape, BF16),
            shape((1, owned, width), BF16),
            shape((1, owned, width), BF16),
            shape((1, owned, width), BF16),
        ),
        in_specs=[vmem, vmem, vmem, vmem, hbm, hbm, hbm],
        out_specs=[vmem] * 2 + [hbm] * 3,
        scratch_shapes=[
            pltpu.VMEM((sources, toks, width + LANES), BF16),
            pltpu.VMEM((sources, toks, width), BF16),
            pltpu.VMEM((hid, width), BF16),
            pltpu.VMEM((hid, width), BF16),
            pltpu.VMEM((width, hid), BF16),
            pltpu.VMEM((hid, width), BF16),
            pltpu.VMEM((tiles, 256, rows), F32),
            pltpu.VMEM((tiles, 256, rows), F32),
            pltpu.VMEM((2, rows, width), BF16),
            pltpu.VMEM((sources // GROUP, GROUP * cap, GROUP * toks), BF16),
            pltpu.VMEM((3, hid, rows), BF16),
            pltpu.VMEM((rows, hid), BF16),
            pltpu.VMEM((rows, hid), BF16),
            pltpu.VMEM((rows, width + LANES), BF16),
            pltpu.VMEM((rows, width + LANES), BF16),
            pltpu.VMEM((2, parts, owned, cut), BF16),
            pltpu.VMEM((ring_size - 1, 2, parts, owned, cut), BF16),
            dma((x_copies,)),
            dma((sources,)),
            dma((c_copies,)),
            dma((sources,)),
            dma((sources,)),
            dma((sources,)),
            dma((ring_size - 1, 2, parts)),
            dma((ring_size - 1, 2, parts)),
            dma((2, parts)),
            dma((4,)),
        ],
        compiler_params=pltpu.CompilerParams(
            collective_id=0, has_side_effects=True, vmem_limit_bytes=60 << 20
        ),
    )(tokens, ids, gates, cotangent, w_gate, w_up, w_down)


def settle_kernel(count, *refs):
    ins, outs, sem = refs[:count], refs[count : 2 * count], refs[2 * count]
    copies = [pltpu.make_async_copy(ins[i], outs[i], sem.at[i]) for i in range(count)]
    for copy in copies:
        copy.start()
    for copy in copies:
        copy.wait()


def settle(*arrays):
    count = len(arrays)
    hbm = pl.BlockSpec(memory_space=pl.ANY)
    vmem = pl.BlockSpec(memory_space=pltpu.VMEM)
    return pl.pallas_call(
        functools.partial(settle_kernel, count),
        out_shape=tuple(jax.ShapeDtypeStruct(a.shape, a.dtype) for a in arrays),
        in_specs=[hbm] * count,
        out_specs=[vmem] * count,
        scratch_shapes=[pltpu.SemaphoreType.DMA((count,))],
        compiler_params=pltpu.CompilerParams(vmem_limit_bytes=60 << 20),
    )(*arrays)


def body(tokens, expert_ids, gate_weights, cotangent, w_gate, w_up, w_down):
    tok_rows, top_count = expert_ids.shape
    experts = lax.axis_size("expert")
    cap = min(tok_rows, 2 * tok_rows * top_count // experts)
    token_grad, gate_grad, grad_down_t, grad_gate, grad_up = expert_call(
        tokens, expert_ids.T, gate_weights.T, cotangent, w_gate, w_up, w_down, cap
    )
    token_grad, gate_grad, grad_gate, grad_up, grad_down_t = settle(
        token_grad, gate_grad, grad_gate, grad_up, grad_down_t
    )
    return (token_grad, gate_grad.T, grad_gate, grad_up, grad_down_t)


def solution(mesh):
    rows = P(("expert", "dp"), None)
    whole = P("expert", None, None)
    split = P("expert", "dp", None)
    return jax.shard_map(
        body,
        mesh=mesh,
        in_specs=(rows, rows, rows, rows, whole, whole, whole),
        out_specs=(rows, rows, split, split, split),
        check_vma=False,
    )
```

```python
import functools

import jax
import jax.numpy as jnp
from jax import lax
from jax.experimental import pallas as pl
from jax.experimental.pallas import tpu as pltpu
from jax.sharding import PartitionSpec as P

F32 = jnp.float32
BF16 = jnp.bfloat16
LANES = 128
MESH = pl.DeviceIdType.MESH
YS, ZS = 4, 8
GROUP = 2 * YS


def contract_last(left, right):
    return lax.dot_general(
        left, right, (((1,), (1,)), ((), ())), preferred_element_type=F32
    )


def contract_first(left, right):
    return lax.dot_general(
        left, right, (((0,), (0,)), ((), ())), preferred_element_type=F32
    )


def dot(left, right):
    return jnp.dot(left, right, preferred_element_type=F32)


def expert_kernel(
    cap,
    tok_ref,
    ids_ref,
    gates_ref,
    cot_ref,
    wg_hbm,
    wu_hbm,
    wd_hbm,
    tok_out,
    gate_out,
    down_out,
    gate_mat_out,
    up_out,
    xg,
    cg,
    wg,
    wu,
    wd,
    wd_t,
    pre_gate,
    pre_up,
    pair,
    gate_hot,
    left,
    d_gate,
    d_up,
    back,
    home_ref,
    first,
    ring,
    x_send,
    x_recv,
    c_send,
    c_recv,
    home_send,
    home_recv,
    ring_send,
    ring_recv,
    out_sem,
    w_sem,
):
    e = lax.axis_index("expert")
    dp = lax.axis_index("dp")
    core = e % 2
    z = (e // 2) % ZS
    y = e // (2 * ZS)
    turn = 1 - 2 * core
    toks, width = tok_ref.shape
    sources = xg.shape[0]
    hid = wg.shape[0]
    rows = sources * cap
    half_rows = rows // 2
    far = ZS // 2
    group_tokens = GROUP * toks
    group_rows = GROUP * cap
    ring_size = ring.shape[0] + 1
    owned = hid // ring_size
    parts = ring.shape[2]
    cut = ring.shape[4]
    top = ids_ref.shape[0]

    loads = [
        pltpu.make_async_copy(src.at[0], dst, w_sem.at[i])
        for i, (src, dst) in enumerate(((wd_hbm, wd), (wg_hbm, wg), (wu_hbm, wu)))
    ]
    for load in loads:
        load.start()

    def device(j, k, q):
        return ((y + turn * j + YS) % YS * ZS + (z + turn * k + ZS) % ZS) * 2 + (core + q) % 2

    def spot(j, k, q=0):
        return ((k + far // 2) % ZS * YS + j % YS) * 2 + q

    hops = {
        "ahead": (device(0, 1, 0), 0, -1),
        "behind": (device(0, -1, 0), 0, 1),
        "up": (device(1, 0, 0), -1, 0),
        "down": (device(-1, 0, 0), 1, 0),
    }
    partner = device(0, 0, 1)
    ring_to = ((dp + 1) % ring_size, (dp + ring_size - 1) % ring_size)
    barrier = pltpu.get_barrier_semaphore()
    greeted = [(peer, dp) for peer in (*(hop[0] for hop in hops.values()), partner)]
    greeted += [(e, peer) for peer in ring_to]
    for peer in greeted:
        pl.semaphore_signal(barrier, inc=1, device_id=peer, device_id_type=MESH)
    named_here = jnp.concatenate([ids_ref[...].astype(F32), gates_ref[...].astype(F32)], axis=0)
    unit16 = lax.broadcasted_iota(jnp.int32, (2 * top, LANES), 0) == lax.broadcasted_iota(
        jnp.int32, (2 * top, LANES), 1
    )
    unit16 = jnp.where(unit16, 1.0, 0.0).astype(BF16)
    meta_own = contract_first(named_here.astype(BF16), unit16)
    own = spot(0, 0)
    xg[own, :, :width] = tok_ref[...]
    xg[own, :, width:] = meta_own.astype(BF16)
    cg[own] = cot_ref[...]
    pl.semaphore_wait(barrier, len(greeted))

    sends = []
    used = {"x": 0, "c": 0}

    def push(kind, j, k, ways):
        buf, ssem, rsem = (xg, x_send, x_recv) if kind == "x" else (cg, c_send, c_recv)
        for way in ways:
            if way == "partner":
                peer, there = partner, spot(-j, -k, 1)
            else:
                peer, dj, dk = hops[way]
                there = spot(j + dj, k + dk)
            copy = pltpu.make_async_remote_copy(
                src_ref=buf.at[spot(j, k)],
                dst_ref=buf.at[there],
                send_sem=ssem.at[used[kind]],
                recv_sem=rsem.at[there],
                device_id=(peer, dp),
                device_id_type=MESH,
            )
            copy.start()
            used[kind] += 1
            sends.append(copy)

    def arrived(kind, slot_at):
        buf, ssem, rsem = (xg, x_send, x_recv) if kind == "x" else (cg, c_send, c_recv)
        pltpu.make_async_remote_copy(
            src_ref=buf.at[slot_at],
            dst_ref=buf.at[slot_at],
            send_sem=ssem.at[0],
            recv_sem=rsem.at[slot_at],
            device_id=(partner, dp),
            device_id_type=MESH,
        ).wait_recv()

    def along_z(k):
        if -far < k < 0:
            return ["ahead"]
        return ["behind"] if 0 < k < far - 1 else []

    def x_step(j, k):
        arrived("x", spot(j, k))
        ways = ["ahead", "behind"] if k == 0 else along_z(k)
        if k == 0 and j == -1:
            ways = ["up", *ways]
        push("x", j, k, [*ways, "partner"])

    def c_step(k):
        arrived("c", spot(0, k))
        push("c", 0, k, [*along_z(k), "up", "down", "partner"])

    def c_hand(j, k):
        arrived("c", spot(j, k))
        push("c", j, k, ["up", "partner"] if j == -1 else ["partner"])

    before = lax.broadcasted_iota(jnp.int32, (group_tokens, group_tokens), 0)
    after = lax.broadcasted_iota(jnp.int32, (group_tokens, group_tokens), 1)
    earlier = ((before < after) & (before // toks == after // toks)).astype(F32).astype(BF16)
    row = lax.broadcasted_iota(jnp.int32, (group_rows, group_tokens), 0)
    col = lax.broadcasted_iota(jnp.int32, (group_rows, group_tokens), 1)
    own_block = row // cap == col // toks
    slot = (row % cap).astype(F32)
    lane = lax.broadcasted_iota(jnp.int32, (group_tokens, LANES), 1)
    mine = e.astype(F32)
    ones = jnp.ones((8, LANES), BF16)
    tile = 256
    tiles = hid // tile

    def select(g):
        block = pl.ds(g * GROUP, GROUP)
        meta = xg[block, :, width:].reshape(group_tokens, LANES).astype(F32)
        named = (meta == mine) & (lane < top)
        gate = jnp.where(named, pltpu.roll(meta, LANES - top, 1), 0.0).astype(BF16)
        hits = jnp.where(named, 1.0, 0.0).astype(BF16)
        here = contract_last(ones, hits)
        rank = dot(here.astype(BF16), earlier)
        weight = contract_last(ones, gate)[0:1]
        chosen = own_block & (here[0:1] > 0.5) & (rank[0:1] == slot)
        return chosen, weight

    def handed(kind, p):
        for j in range(YS):
            arrived(kind, spot(j, p - far // 2, 1))

    def pick_x(p):
        handed("x", p)
        chosen, weight = select(p)
        tokens = xg[p * GROUP : (p + 1) * GROUP, :, :width].reshape(group_tokens, width)
        one_hot = jnp.where(chosen, 1.0, 0.0).astype(BF16)
        gate_hot[p] = jnp.where(chosen, weight, 0.0).astype(BF16)
        span = pl.ds(p * group_rows, group_rows)
        pair[0, span, :] = dot(one_hot, tokens).astype(BF16)

    def pick_c(p):
        handed("c", p)
        cots = cg[p * GROUP : (p + 1) * GROUP].reshape(group_tokens, width)
        span = pl.ds(p * group_rows, group_rows)
        pair[1, span, :] = dot(gate_hot[p], cots).astype(BF16)

    def take_x(half):
        span = pl.ds(half * half_rows, half_rows)

        def forward(n, _):
            cols = pl.ds(pl.multiple_of(n * tile, tile), tile)
            pre_gate[n, :, span] = contract_last(wg[cols, :], pair[0, span, :])
            pre_up[n, :, span] = contract_last(wu[cols, :], pair[0, span, :])
            return 0

        lax.fori_loop(0, tiles, forward, 0)

    def take_c(half):
        span = pl.ds(half * half_rows, half_rows)

        def grads(n, score):
            cols = pl.ds(pl.multiple_of(n * tile, tile), tile)
            d_hidden = contract_last(wd_t[cols, :], pair[1, span, :])
            gate, up = pre_gate[n, :, span], pre_up[n, :, span]
            sig = jax.nn.sigmoid(gate)
            act = gate * sig
            hidden = (act * up).astype(BF16)
            left[0, cols, span] = hidden
            left[1, cols, span] = (
                d_hidden * up * sig * (1.0 + gate * (1.0 - sig))
            ).astype(BF16)
            left[2, cols, span] = (d_hidden * act).astype(BF16)
            return score + jnp.sum(hidden.astype(F32) * d_hidden, axis=0, keepdims=True)

        score = lax.fori_loop(0, tiles, grads, jnp.zeros((1, half_rows), F32))
        high = score.astype(BF16).astype(F32)
        which = lax.broadcasted_iota(jnp.int32, (8, half_rows), 0)
        both = jnp.where(which == 0, high, jnp.where(which == 1, score - high, 0.0))
        unit = lax.broadcasted_iota(jnp.int32, (8, LANES), 0) == lax.broadcasted_iota(
            jnp.int32, (8, LANES), 1
        )
        unit = jnp.where(unit, 1.0, 0.0).astype(BF16)
        back[span, width:] = contract_first(both.astype(BF16), unit).astype(BF16)

    def turn_down(c):
        span = pl.ds(c * tile, tile)
        wd_t[:, span] = wd[span, :].T

    push("x", 0, 0, ["up", "down", "ahead", "behind"])
    push("c", 0, 0, ["ahead", "behind", "up", "down"])
    push("x", 0, 0, ["partner"])
    push("c", 0, 0, ["partner"])
    turns = list(range(width // tile))
    for j in (-1, 1, -2):
        x_step(j, 0)

    def both_ways(k):
        return (0,) if k == 0 else (-k, k) if k < far else (-k,)

    def c_turn(at):
        for k in range(far + 1):
            if k > 0 and at == k + 1:
                for way in both_ways(k):
                    c_step(way)
            if at == k + 3:
                for way in both_ways(k):
                    c_hand(-1, way)
                    c_hand(1, way)
            if at == k + 4:
                for way in both_ways(k):
                    c_hand(-2, way)

    for k in range(1, far + 1):
        for h, js in enumerate(((0, -1), (1, -2))):
            c_turn(2 * k + h)
            if k == far - 1 and h == 0:
                for p in (1, 2, 3):
                    pick_c(p)
            for j in js:
                for way in both_ways(k):
                    x_step(j, way)
                if turns and k > 1:
                    turn_down(turns.pop())
        if k == 1:
            for load in loads:
                load.wait()
            for p in (1, 2, 3):
                pick_x(p)
        if k == 2:
            pick_x(0)
            pick_x(4)
            take_x(0)
        if k == far - 1:
            while turns:
                turn_down(turns.pop())
            pick_x(5)
            pick_x(7)
            pick_c(0)
            pick_c(4)
    take_c(0)
    pick_c(5)
    pick_c(7)
    pick_x(6)
    take_x(1)
    pick_c(6)
    take_c(1)

    owners = [
        [(dp + ring_size - 1 - s) % ring_size for s in range(ring_size)],
        [(dp + 1 + s) % ring_size for s in range(ring_size)],
    ]

    def partial(owner, side, i):
        per = parts // 3
        m = i // per
        cols = pl.ds(pl.multiple_of((side * per + i % per) * cut, cut), cut)
        lhs = left[m, pl.ds(pl.multiple_of(owner * owned, 16), owned), :]
        return dot(lhs, pair[(3 - m) // 3, :, cols]), m, cols

    def ring_copy(s, side, i):
        return pltpu.make_async_remote_copy(
            src_ref=first.at[side, i] if s == 0 else ring.at[s - 1, side, i],
            dst_ref=ring.at[s, side, i],
            send_sem=ring_send.at[s, side, i],
            recv_sem=ring_recv.at[s, side, i],
            device_id=(e, ring_to[side]),
            device_id_type=MESH,
        )

    def ring_start(i, _):
        for side in range(2):
            first[side, i] = partial(owners[side][0], side, i)[0].astype(BF16)
            ring_copy(0, side, i).start()
        return 0

    lax.fori_loop(0, parts, ring_start, 0)

    for n in range(tiles):
        span = pl.ds(n * tile, tile)
        d_gate[:, span] = left[1, span, :].T
        d_up[:, span] = left[2, span, :].T

    def backward(n, _):
        cols = pl.ds(pl.multiple_of(n * tile, tile), tile)
        total = dot(d_gate[...], wg[:, cols]) + dot(d_up[...], wu[:, cols])
        back[:, cols] = total.astype(BF16)
        return 0

    lax.fori_loop(0, width // tile, backward, 0)

    def home_copy(i):
        k, j, q = i // (2 * YS) - far // 2, i // 2 % YS, i % 2
        return pltpu.make_async_remote_copy(
            src_ref=back.at[pl.ds(pl.multiple_of(i * cap, cap), cap), :],
            dst_ref=home_ref.at[pl.ds(pl.multiple_of(e * cap, cap), cap), :],
            send_sem=home_send.at[i],
            recv_sem=home_recv.at[e],
            device_id=(device(j, k, q), dp),
            device_id_type=MESH,
        )

    def go_home(i, _):
        home_copy(i).start()
        return 0

    lax.fori_loop(0, own, go_home, 0)
    lax.fori_loop(own + 1, sources, go_home, 0)
    kept = pltpu.make_async_copy(
        back.at[pl.ds(own * cap, cap), :],
        home_ref.at[pl.ds(pl.multiple_of(e * cap, cap), cap), :],
        w_sem.at[3],
    )
    kept.start()

    expert_lane = lax.broadcasted_iota(jnp.int32, (toks, sources), 1).astype(F32)
    names = sum(jnp.where(meta_own[:, k : k + 1] == expert_lane, 1.0, 0.0) for k in range(top))
    sooner = lax.broadcasted_iota(jnp.int32, (toks, toks), 1) < lax.broadcasted_iota(
        jnp.int32, (toks, toks), 0
    )
    place = dot(jnp.where(sooner, 1.0, 0.0).astype(BF16), names.astype(BF16))
    home_row = lax.broadcasted_iota(jnp.int32, (sources, rows), 1) // cap
    spread = home_row == lax.broadcasted_iota(jnp.int32, (sources, rows), 0)
    spread = jnp.where(spread, 1.0, 0.0).astype(BF16)
    row_lane = lax.broadcasted_iota(jnp.int32, (toks, rows), 1)
    token_map = (dot(names.astype(BF16), spread) > 0.5) & (
        dot(place.astype(BF16), spread) == (row_lane % cap).astype(F32)
    )
    row_expert = (row_lane // cap).astype(F32)

    for s in range(1, ring_size - 1):

        def ring_on(i, _):
            for side in range(2):
                ring_copy(s - 1, side, i).wait_recv()
                mine_now = partial(owners[side][s], side, i)[0]
                ring[s - 1, side, i] = (mine_now + ring[s - 1, side, i].astype(F32)).astype(BF16)
                ring_copy(s, side, i).start()
            return 0

        lax.fori_loop(0, parts, ring_on, 0)
        if s == 1:
            for copy in sends:
                copy.wait_send()

    last = ring_size - 2

    def came_home(i, _):
        peer = (e + i) % sources
        pltpu.make_async_remote_copy(
            src_ref=back.at[pl.ds(0, cap), :],
            dst_ref=home_ref.at[pl.ds(pl.multiple_of(peer * cap, cap), cap), :],
            send_sem=home_send.at[0],
            recv_sem=home_recv.at[peer],
            device_id=(peer, dp),
            device_id_type=MESH,
        ).wait_recv()
        return 0

    kept.wait()
    lax.fori_loop(1, sources, came_home, 0)
    one_map = jnp.where(token_map, 1.0, 0.0).astype(BF16)

    def combine(n, _):
        cols = pl.ds(pl.multiple_of(n * tile, tile), tile)
        tok_out[:, cols] = dot(one_map, home_ref[:, cols]).astype(BF16)
        return 0

    lax.fori_loop(0, width // tile, combine, 0)
    unit8 = lax.broadcasted_iota(jnp.int32, (8, LANES), 0) == lax.broadcasted_iota(
        jnp.int32, (8, LANES), 1
    )
    scores = contract_last(jnp.where(unit8, 1.0, 0.0).astype(BF16), home_ref[:, width:])
    scores = scores.astype(BF16)
    which_k = lax.broadcasted_iota(jnp.int32, (top, toks), 0)
    gate_sum = jnp.zeros((top, toks), F32)
    for k in range(top):
        mine_k = token_map & (meta_own[:, k : k + 1] == row_expert)
        found = contract_last(scores, jnp.where(mine_k, 1.0, 0.0).astype(BF16))
        gate_sum = jnp.where(which_k == k, found[0:1] + found[1:2], gate_sum)
    gate_out[...] = (gate_sum / gates_ref[...].astype(F32)).astype(BF16)

    def left_home(i, _):
        home_copy(i).wait_send()
        return 0

    lax.fori_loop(0, own, left_home, 0)
    lax.fori_loop(own + 1, sources, left_home, 0)

    def ring_left(s):
        def ring_sent(i, _):
            for side in range(2):
                ring_copy(s, side, i).wait_send()
            return 0

        lax.fori_loop(0, parts, ring_sent, 0)

    for s in range(last):
        ring_left(s)
    per = parts // 3

    def out_copy(out, side, i, cols):
        return pltpu.make_async_copy(
            ring.at[last, side, i], out.at[0, :, cols], out_sem.at[side, i]
        )

    for m, out in enumerate((down_out, gate_mat_out, up_out)):

        def ring_end(i, _):
            for side in range(2):
                ring_copy(last, side, m * per + i).wait_recv()
                total, _m, cols = partial(dp, side, m * per + i)
                sofar = ring[last, side, m * per + i].astype(F32)
                ring[last, side, m * per + i] = (total + sofar).astype(BF16)
                out_copy(out, side, m * per + i, cols).start()
            return 0

        lax.fori_loop(0, per, ring_end, 0)

    for m, out in enumerate((down_out, gate_mat_out, up_out)):

        def out_done(i, _):
            for side in range(2):
                cols = pl.ds(pl.multiple_of((side * per + i) * cut, cut), cut)
                out_copy(out, side, m * per + i, cols).wait()
            return 0

        lax.fori_loop(0, per, out_done, 0)

    ring_left(last)


def expert_call(tokens, ids, gates, cotangent, w_gate, w_up, w_down, cap):
    toks, width = tokens.shape
    sources = lax.axis_size("expert")
    ring_size = lax.axis_size("dp")
    hid = w_gate.shape[1]
    rows = sources * cap
    tiles = hid // 256
    owned = hid // ring_size
    per = 2
    cut = width // (2 * per)
    parts = 3 * per
    far = ZS // 2
    x_copies = 5 + 3 * (YS - 1) + 1 + YS * (4 * far - 4)
    c_copies = 5 + 3 * (2 * far - 1) + 2 * far - 3 + YS * ZS
    vmem = pl.BlockSpec(memory_space=pltpu.VMEM)
    hbm = pl.BlockSpec(memory_space=pl.ANY)
    shape = jax.ShapeDtypeStruct
    dma = pltpu.SemaphoreType.DMA
    return pl.pallas_call(
        functools.partial(expert_kernel, cap),
        out_shape=(
            shape((toks, width), BF16),
            shape(gates.shape, BF16),
            shape((1, owned, width), BF16),
            shape((1, owned, width), BF16),
            shape((1, owned, width), BF16),
        ),
        in_specs=[vmem, vmem, vmem, vmem, hbm, hbm, hbm],
        out_specs=[vmem] * 2 + [hbm] * 3,
        scratch_shapes=[
            pltpu.VMEM((sources, toks, width + LANES), BF16),
            pltpu.VMEM((sources, toks, width), BF16),
            pltpu.VMEM((hid, width), BF16),
            pltpu.VMEM((hid, width), BF16),
            pltpu.VMEM((width, hid), BF16),
            pltpu.VMEM((hid, width), BF16),
            pltpu.VMEM((tiles, 256, rows), F32),
            pltpu.VMEM((tiles, 256, rows), F32),
            pltpu.VMEM((2, rows, width), BF16),
            pltpu.VMEM((sources // GROUP, GROUP * cap, GROUP * toks), BF16),
            pltpu.VMEM((3, hid, rows), BF16),
            pltpu.VMEM((rows, hid), BF16),
            pltpu.VMEM((rows, hid), BF16),
            pltpu.VMEM((rows, width + LANES), BF16),
            pltpu.VMEM((rows, width + LANES), BF16),
            pltpu.VMEM((2, parts, owned, cut), BF16),
            pltpu.VMEM((ring_size - 1, 2, parts, owned, cut), BF16),
            dma((x_copies,)),
            dma((sources,)),
            dma((c_copies,)),
            dma((sources,)),
            dma((sources,)),
            dma((sources,)),
            dma((ring_size - 1, 2, parts)),
            dma((ring_size - 1, 2, parts)),
            dma((2, parts)),
            dma((4,)),
        ],
        compiler_params=pltpu.CompilerParams(
            collective_id=0, has_side_effects=True, vmem_limit_bytes=60 << 20
        ),
    )(tokens, ids, gates, cotangent, w_gate, w_up, w_down)


def settle_kernel(count, *refs):
    ins, outs, sem = refs[:count], refs[count : 2 * count], refs[2 * count]
    copies = [pltpu.make_async_copy(ins[i], outs[i], sem.at[i]) for i in range(count)]
    for copy in copies:
        copy.start()
    for copy in copies:
        copy.wait()


def settle(*arrays):
    count = len(arrays)
    hbm = pl.BlockSpec(memory_space=pl.ANY)
    vmem = pl.BlockSpec(memory_space=pltpu.VMEM)
    return pl.pallas_call(
        functools.partial(settle_kernel, count),
        out_shape=tuple(jax.ShapeDtypeStruct(a.shape, a.dtype) for a in arrays),
        in_specs=[hbm] * count,
        out_specs=[vmem] * count,
        scratch_shapes=[pltpu.SemaphoreType.DMA((count,))],
        compiler_params=pltpu.CompilerParams(vmem_limit_bytes=60 << 20),
    )(*arrays)


def body(tokens, expert_ids, gate_weights, cotangent, w_gate, w_up, w_down):
    tok_rows, top_count = expert_ids.shape
    experts = lax.axis_size("expert")
    cap = min(tok_rows, 2 * tok_rows * top_count // experts)
    token_grad, gate_grad, grad_down_t, grad_gate, grad_up = expert_call(
        tokens, expert_ids.T, gate_weights.T, cotangent, w_gate, w_up, w_down, cap
    )
    token_grad, gate_grad, grad_gate, grad_up, grad_down_t = settle(
        token_grad, gate_grad, grad_gate, grad_up, grad_down_t
    )
    return (token_grad, gate_grad.T, grad_gate, grad_up, grad_down_t)


def solution(mesh):
    rows = P(("expert", "dp"), None)
    whole = P("expert", None, None)
    split = P("expert", "dp", None)
    return jax.shard_map(
        body,
        mesh=mesh,
        in_specs=(rows, rows, rows, rows, whole, whole, whole),
        out_specs=(rows, rows, split, split, split),
        check_vma=False,
    )
```
